512 devices in a mesh: blk: 8 (over z_hi, y), expert: 32 (over z_lo, x), tp: 2 (over core).
Axes of the slice: x: 4, y: 4, z: 16 (z_hi: 2, z_lo: 8; z = z_hi * 8 + z_lo), core: 2. Of those that a mesh axis runs over, the one named last changes fastest.
Arguments:
- tokens: bfloat16 [4096, 1536], P(('blk', 'expert')), may hold values from -6 to 6
- w_query: bfloat16 [1536, 1536], P('expert', 'tp'), may hold values from -0.15625 to 0.15625
- w_key: bfloat16 [1536, 512], P('expert', 'tp'), may hold values from -2.5 to 2.5
- w_value: bfloat16 [1536, 512], P('expert', 'tp'), may hold values from -0.15625 to 0.15625
- w_out: bfloat16 [1536, 1536], P('tp', 'expert'), may hold values from -0.15625 to 0.15625
- cache_keys: bfloat16 [64, 1024, 512], P('expert', 'blk', 'tp'), may hold values from -3840 to 3840, as said below
- cache_values: bfloat16 [64, 1024, 512], P('expert', 'blk', 'tp'), may hold values from -6 to 6
- parents: int32 [64, 64], P('expert'), may hold values from -1 to 62, as said below
- lengths: int32 [64], P('expert'), may hold values from 1 to 960, as said below
- accepted_leaf: int32 [64], P('expert'), may hold values from 0 to 63
- routes: int32 [4096, 8], P(('blk', 'expert')), may hold values from 0 to 31, all different within a row; in each aligned block of 16 rows (0 to 15, 16 to 31, ...) at most 6 rows name the same one
- route_weight: float32 [4096, 8], P(('blk', 'expert')), may hold values from 0.05 to 0.3
- w_gateup: bfloat16 [32, 1536, 2, 512], P('expert', None, None, 'tp'), may hold values from -0.15625 to 0.15625
- w_down: bfloat16 [32, 512, 1536], P('expert', 'tp'), may hold values from -0.25 to 0.25
Outputs:
- attended: bfloat16 [4096, 1536], P(('blk', 'expert'))
- expert_mix: bfloat16 [4096, 1536], P(('blk', 'expert'))
- new_keys: bfloat16 [64, 1024, 512], P('expert', 'blk', 'tp')
- new_values: bfloat16 [64, 1024, 512], P('expert', 'blk', 'tp')
The draws below stay inside these ranges and needn't reach their ends.
Inputs may be any that keep to these rules, and one draw needn't show every extreme that they name: `cache_keys`: entries are finite and within the range. `parents`: token 0 of each request is the root, with parent -1; every other token's parent is a token of the same request with a lower index. `lengths`: each request's cache leaves room for its whole tree; some request has exactly 960 cached positions. `routes`: within the rows of one device (aligned blocks of 16 rows) no expert is named by more than 6 rows, a bound that some block reaches; the experts of a row differ.
All inputs are finite; a program needn't handle non-finite values.
Results may differ from the reference program's by a relative error of at most 0.02.
Values may be sent and summed in bfloat16 or wider, within the bound.
A program may use at most 64 MiB of HBM per device.

```python
import math
import jax
import jax.numpy as jnp
import numpy as np
from jax import lax

D = 1536
QH = 24
KVH = 8
HD = 64
FF = 512
EXPERTS = 32
TOPK = 8
TREE = 64
REQS = 64
CACHE = 1024
TB = 8
TOKS = 4096
ROWS = 16
CAP = 6
N_BLK = 8
N_EXPERT = 32


def draw_cache_keys(key, part):
    base = jax.random.truncated_normal(key, -6.0, 6.0, (REQS, CACHE, KVH * HD), jnp.float32) * 16.0
    return base.astype(jnp.bfloat16)


def draw_parents(key, part):
    index_row = jnp.arange(TREE, dtype=jnp.int32)
    chained = jax.random.randint(jax.random.fold_in(key, 1), (REQS, TREE), 0, 2)
    anywhere = jax.random.randint(jax.random.fold_in(key, 2), (REQS, TREE), 0, jnp.maximum(index_row, 1)[None, :])
    chosen = jnp.where(chained == 1, index_row[None, :] - 1, anywhere)
    return jnp.where(index_row[None, :] == 0, -1, chosen).astype(jnp.int32)


def draw_lengths(key, part):
    room = CACHE - TREE
    base = jax.random.randint(jax.random.fold_in(key, 1), (REQS,), 1, room + 1)
    longest = jax.random.randint(jax.random.fold_in(key, 2), (), 0, REQS)
    return jnp.where(jnp.arange(REQS, dtype=jnp.int32) == longest, room, base).astype(jnp.int32)


def set_ends(array, key, smallest, largest):
    dims = array.shape
    place = [jax.random.randint(jax.random.fold_in(key, axis), (), 0, dims[axis]) for axis in range(len(dims))]
    array = array.at[tuple(place)].set(smallest)
    longest = dims.index(max(dims))
    place[longest] = (place[longest] + 1) % dims[longest]
    return array.at[tuple(place)].set(largest)


def steps_of(key, shape, split, smallest, top_value):
    level = 1.0
    for dim, blocks in split:
        heights = jax.random.uniform(jax.random.fold_in(jax.random.fold_in(key, 6), dim), (blocks,), jnp.float32, smallest / len(split), top_value / len(split))
        level = level * jnp.repeat(jnp.exp(heights), shape[dim] // blocks).reshape((-1,) + (1,) * (len(shape) - 1 - dim))
    return level


def routed_block(own_key, own, number, rows, amount, top, reach, lean):
    order = jax.random.permutation(own_key, amount)
    heavy_load, common = load_shares(amount, rows * top, reach, lean, True), load_shares(amount, rows * top, reach, lean, False)
    places = jnp.arange(amount)

    def named(sizes, turn):
        used = int((sizes > 0).sum())
        fixed = max(1, used // 4)
        shifted = fixed + (places - fixed + turn * (used - fixed)) % max(1, amount - fixed)
        return jnp.zeros((amount,), jnp.int32).at[order[jnp.where(places < fixed, places, shifted)]].set(jnp.asarray(sizes, jnp.int32))

    sizes = jnp.where(number % 4 == 0, named(heavy_load, number // 4), named(common, number - number // 4 - 1))
    mixed = jax.random.permutation(jax.random.fold_in(own, 3), amount)
    donor, sink = mixed[0:amount // 2 * 2:2], mixed[1:amount // 2 * 2:2]
    room = jnp.minimum(sizes[donor] - 1, reach - sizes[sink]) // 2
    room = jnp.where((donor == order[0]) | (sink == order[0]) | (sizes[sink] == 0), 0, jnp.maximum(room, 0))
    shifted = jax.random.randint(jax.random.fold_in(own, 4), (amount // 2,), 0, 1 << 20) % (room + 1)
    sizes = sizes.at[donor].add(-shifted).at[sink].add(shifted)
    items = jnp.searchsorted(jnp.cumsum(sizes), jnp.arange(rows * top), side="right").astype(jnp.int32)
    listing = items.reshape(top, rows).T
    listing = listing[jax.random.permutation(jax.random.fold_in(own, 1), rows)]
    turn = jax.random.randint(jax.random.fold_in(own, 2), (rows, 1), 0, top)
    return jnp.take_along_axis(listing, (jnp.arange(top)[None, :] + turn) % top, axis=1)


def load_shares(count, total, bound, lean, full):
    weights = [(1 << 20) // math.isqrt(standing ** lean) + 1 for standing in range(1, count + 1)]
    largest = bound if full else min(bound, max(-(-total // count), total * weights[0] // sum(weights)))
    least = 1 if total - largest >= count - 1 else 0
    given, spare = [largest] + [least] * (count - 1), total - largest - least * (count - 1)
    while spare > 0:
        free = [i for i in range(1, count) if given[i] < largest] or [i for i in range(1, count) if given[i] < bound]
        mass, remaining = sum([weights[i] for i in free]), spare
        for i in free:
            addition = min(bound - given[i], max(1, remaining * weights[i] // mass), spare)
            given[i] = given[i] + addition
            spare = spare - addition
    return np.array(given)


def gaussian(rng, extent, deviation, bound, shards=(), kind=jnp.bfloat16):
    level = steps_of(rng, extent, shards, -0.22, 0.18) if shards else 1.0
    array = jax.random.normal(rng, extent, jnp.float32) * deviation * level
    return jnp.minimum(jnp.maximum(array, -bound), bound).astype(kind)


def setup_inputs(seed: int = 0) -> dict:
    streams_of = jax.random.split(jax.random.key(seed), 15)
    tokens = gaussian(streams_of[0], (TOKS, D), 1.0, 6.0, ((0, 256),))
    w_query = gaussian(streams_of[1], (D, QH * HD), D ** -0.5, 0.15625, ((0, 32), (1, 2)))
    w_key = gaussian(streams_of[2], (D, KVH * HD), (max(1, D // 256)) ** -0.5, 2.5, ((0, 32), (1, 2)))
    w_value = gaussian(streams_of[3], (D, KVH * HD), D ** -0.5, 0.15625, ((0, 32), (1, 2)))
    w_out = gaussian(streams_of[4], (QH * HD, D), (QH * HD) ** -0.5, 0.15625, ((0, 2), (1, 32)))
    cache_keys = draw_cache_keys(jax.random.fold_in(streams_of[14], 71), 0)
    cache_values = gaussian(streams_of[6], (REQS, CACHE, KVH * HD), 1.0, 6.0, ((0, 32), (1, 8), (2, 2)))
    parents = draw_parents(jax.random.fold_in(streams_of[14], 71), 0)
    lengths = draw_lengths(jax.random.fold_in(streams_of[14], 71), 0)
    accepted_leaf = set_ends(jax.random.randint(streams_of[9], (REQS,), 0, TREE), jax.random.fold_in(streams_of[9], 1), 0, TREE - 1).astype(jnp.int32)
    routes_keys = jax.random.split(jax.random.fold_in(streams_of[10], 1), TOKS // ROWS)
    routes_turns = jax.random.permutation(jax.random.fold_in(streams_of[10], 3), TOKS // ROWS)
    routes = jax.vmap(lambda own, number: routed_block(jax.random.fold_in(streams_of[10], 2), own, number, ROWS, EXPERTS, TOPK, CAP, 2))(routes_keys, routes_turns).reshape((TOKS, TOPK))
    route_weight = jnp.clip(0.05 + 0.25 * jax.random.uniform(streams_of[11], (TOKS, TOPK), jnp.float32) ** steps_of(streams_of[11], (TOKS, TOPK), ((0, 256),), -0.2, 0.2), 0.05, 0.3)
    w_gateup = gaussian(streams_of[12], (EXPERTS, D, 2, FF), D ** -0.5, 0.15625, ((0, 32), (3, 2)))
    w_down = gaussian(streams_of[13], (EXPERTS, FF, D), FF ** -0.5, 0.25, ((0, 32), (1, 2)))
    return {"tokens": tokens, "w_query": w_query, "w_key": w_key, "w_value": w_value, "w_out": w_out, "cache_keys": cache_keys, "cache_values": cache_values, "parents": parents, "lengths": lengths, "accepted_leaf": accepted_leaf, "routes": routes, "route_weight": route_weight, "w_gateup": w_gateup, "w_down": w_down}


score_scale = 0.015625
residual_scale = 0.22
masked_score = -1e+30
rope_base = 10000.0

def ancestry(parents):
    tree_size = parents.shape[-1]
    columns = jnp.arange(tree_size, dtype=jnp.int32)
    parent_map = (parents[..., :, None] == columns).astype(jnp.float32)
    reached = jnp.minimum(jnp.eye(tree_size, dtype=jnp.float32) + parent_map, 1.0)
    for squaring in range(tree_size.bit_length()):
        longer = jnp.einsum('rij,rjk->rik', reached, reached, precision=lax.Precision.HIGHEST)
        reached = jnp.minimum(reached + longer, 1.0)
    return reached

def rms_norm(values):
    widened = values.astype(jnp.float32)
    scale_row = lax.rsqrt(lax.optimization_barrier(jnp.mean(widened * widened, axis=-1, keepdims=True)) + 1e-06)
    return (widened * scale_row).astype(jnp.bfloat16)

def rotary(values, positions):
    half_size = values.shape[-1] // 2
    frequency = rope_base ** (-(jnp.arange(half_size, dtype=jnp.float32) / half_size))
    angles = positions.astype(jnp.float32)[:, None] * frequency[None, :]
    cosine_part = jnp.cos(angles)[:, None, :]
    sine_part = jnp.sin(angles)[:, None, :]
    first_half = values[..., :half_size]
    second_half = values[..., half_size:]
    return jnp.concatenate([first_half * cosine_part - second_half * sine_part, second_half * cosine_part + first_half * sine_part], -1)

def reference(tokens, w_query, w_key, w_value, w_out, cache_keys, cache_values, parents, lengths, accepted_leaf, routes, route_weight, w_gateup, w_down):
    highest = lax.Precision.HIGHEST
    reached = ancestry(parents)
    depths = (lax.optimization_barrier(jnp.sum(reached, -1)) - 1.0).astype(jnp.int32)
    positions = (lengths[:, None] + depths).reshape(-1)
    by_request = tokens.reshape(N_BLK, REQS, TB, D).transpose(1, 0, 2, 3).reshape(REQS * TREE, D)
    normed = rms_norm(by_request)
    query_all = rotary(jnp.dot(normed, w_query, preferred_element_type=jnp.float32).reshape(REQS * TREE, QH, HD), positions).astype(jnp.bfloat16)
    key_all = rotary(jnp.dot(normed, w_key, preferred_element_type=jnp.float32).reshape(REQS * TREE, KVH, HD), positions).astype(jnp.bfloat16)
    value_all = jnp.dot(normed, w_value, preferred_element_type=jnp.float32).astype(jnp.bfloat16)
    group_size = QH // KVH

    def attend_request(packed):
        query_r, key_r, value_r, cache_k, cache_v, length, reach_r = packed
        key_set = jnp.concatenate([cache_k, key_r], 0).astype(jnp.float32)
        value_set = jnp.concatenate([cache_v, value_r], 0).astype(jnp.float32)
        scores = jnp.einsum('qhgd,khd->qhgk', query_r.astype(jnp.float32), key_set, precision=highest) * score_scale
        cache_ok = jnp.broadcast_to((jnp.arange(CACHE) < length)[None, :], (TREE, CACHE))
        usable = jnp.concatenate([cache_ok, reach_r > 0.5], 1)[:, None, None, :]
        scores = jnp.where(usable, scores, masked_score)
        peak_score = lax.optimization_barrier(jnp.max(scores, -1, keepdims=True))
        weights = jnp.where(usable, jnp.exp(scores - peak_score), 0.0)
        weights = weights / lax.optimization_barrier(jnp.sum(weights, -1, keepdims=True))
        return jnp.einsum('qhgk,khd->qhgd', weights, value_set, precision=highest)
    context = lax.map(attend_request, (query_all.reshape(REQS, TREE, KVH, group_size, HD), key_all.reshape(REQS, TREE, KVH, HD), value_all.reshape(REQS, TREE, KVH, HD), cache_keys.reshape(REQS, CACHE, KVH, HD), cache_values.reshape(REQS, CACHE, KVH, HD), lengths, reached))
    context = context.reshape(REQS * TREE, QH * HD).astype(jnp.bfloat16)
    attended_req = jnp.dot(context, w_out, preferred_element_type=jnp.float32).astype(jnp.bfloat16)
    attended = attended_req.reshape(REQS, N_BLK, TB, D).transpose(1, 0, 2, 3).reshape(TOKS, D)
    mixed_in = rms_norm(tokens.astype(jnp.float32) + residual_scale * attended.astype(jnp.float32))
    flat_route = routes.reshape(-1)
    flat_weight = route_weight.reshape(-1)
    most_rows = N_BLK * N_EXPERT * CAP

    def expert_step(running, expert_id):
        order = jnp.argsort((flat_route != expert_id).astype(jnp.int32), stable=True)[:most_rows]
        live = flat_route[order] == expert_id
        token_idx = order // TOPK
        picked = mixed_in[token_idx]
        gate_up = jnp.dot(picked, w_gateup[expert_id].reshape(D, 2 * FF), preferred_element_type=jnp.float32).reshape(most_rows, 2, FF)
        expert_hidden = (jax.nn.silu(gate_up[:, 0, :]) * gate_up[:, 1, :]).astype(jnp.bfloat16)
        expert_result = jnp.dot(expert_hidden, w_down[expert_id], preferred_element_type=jnp.float32).astype(jnp.bfloat16)
        contrib = jnp.where(live[:, None], flat_weight[order][:, None] * expert_result.astype(jnp.float32), 0.0)
        return (running.at[token_idx].add(contrib), None)
    mixed_total, unused = lax.scan(expert_step, jnp.zeros((TOKS, D), jnp.float32), jnp.arange(EXPERTS, dtype=jnp.int32))
    expert_mix = mixed_total.astype(jnp.bfloat16)
    leaf_pick = (jnp.arange(TREE, dtype=jnp.int32)[None, :] == accepted_leaf[:, None]).astype(jnp.float32)
    path_mask = lax.optimization_barrier(jnp.sum(leaf_pick[:, :, None] * reached, 1))
    target_pos = lengths[:, None] + depths
    cache_pos = jnp.arange(CACHE, dtype=jnp.int32)
    placing = ((cache_pos[None, :, None] == target_pos[:, None, :]) & (path_mask[:, None, :] > 0.5)).astype(jnp.float32)
    written = lax.optimization_barrier(jnp.sum(placing, -1)) > 0.5
    tree_keys = key_all.reshape(REQS, TREE, KVH * HD).astype(jnp.float32)
    tree_values = value_all.reshape(REQS, TREE, KVH * HD).astype(jnp.float32)
    moved_keys = jnp.einsum('rpt,rtc->rpc', placing, tree_keys, precision=highest).astype(jnp.bfloat16)
    moved_values = jnp.einsum('rpt,rtc->rpc', placing, tree_values, precision=highest).astype(jnp.bfloat16)
    new_keys = jnp.where(written[:, :, None], moved_keys, cache_keys)
    new_values = jnp.where(written[:, :, None], moved_values, cache_values)
    return (attended, expert_mix, new_keys, new_values)
```

```python
import jax
import jax.numpy as jnp
from jax import lax
from jax.experimental import pallas as pl
from jax.experimental.pallas import tpu as pltpu
from jax.sharding import PartitionSpec as P

HD = 64


score_scale = 0.015625
residual_scale = 0.22
masked_score = -1e30
rope_base = 10000.0


def passed_along(value, axis, steps):
    count = lax.axis_size(axis)
    pairs = [(source, (source + steps) % count) for source in range(count)]
    return lax.ppermute(value, axis, pairs)


def ancestry(parents):
    tree_size = parents.shape[-1]
    columns = jnp.arange(tree_size, dtype=jnp.int32)
    parent_map = (parents[..., :, None] == columns).astype(jnp.float32)
    reached = jnp.minimum(jnp.eye(tree_size, dtype=jnp.float32) + parent_map, 1.0)
    for squaring in range(tree_size.bit_length()):
        longer = jnp.einsum("rij,rjk->rik", reached, reached, precision=lax.Precision.HIGHEST)
        reached = jnp.minimum(reached + longer, 1.0)
    return reached


def rms_norm(values):
    widened = values.astype(jnp.float32)
    scale_row = lax.rsqrt(jnp.mean(widened * widened, axis=-1, keepdims=True) + 1e-06)
    return (widened * scale_row).astype(jnp.bfloat16)


def rotary(values, positions):
    half_size = values.shape[-1] // 2
    frequency = rope_base ** (-(jnp.arange(half_size, dtype=jnp.float32) / half_size))
    angles = positions.astype(jnp.float32)[:, None] * frequency[None, :]
    cosine_part = jnp.cos(angles)[:, None, :]
    sine_part = jnp.sin(angles)[:, None, :]
    first_half = values[..., :half_size]
    second_half = values[..., half_size:]
    return jnp.concatenate(
        [
            first_half * cosine_part - second_half * sine_part,
            second_half * cosine_part + first_half * sine_part,
        ],
        -1,
    )


def attend_block(query_block, key_block, value_block, usable):
    scores = (
        jnp.einsum("nqhgd,nkhd->nqhgk", query_block, key_block, preferred_element_type=jnp.float32)
        * score_scale
    )
    scores = jnp.where(usable, scores, masked_score)
    peak_score = jnp.max(scores, axis=-1)
    weights = jnp.where(usable, jnp.exp(scores - peak_score[..., None]), 0.0)
    weight_high = weights.astype(jnp.bfloat16)
    weight_low = (weights - weight_high.astype(jnp.float32)).astype(jnp.bfloat16)
    acc_part = jnp.einsum(
        "nqhgk,nkhd->nqhgd", weight_high, value_block, preferred_element_type=jnp.float32
    ) + jnp.einsum("nqhgk,nkhd->nqhgd", weight_low, value_block, preferred_element_type=jnp.float32)
    return (peak_score, jnp.sum(weights, -1), acc_part)


def combine_parts(former, latter):
    peak_score = jnp.maximum(former[0], latter[0])
    scale_one = jnp.exp(former[0] - peak_score)
    scale_two = jnp.exp(latter[0] - peak_score)
    return (
        peak_score,
        former[1] * scale_one + latter[1] * scale_two,
        former[2] * scale_one[..., None] + latter[2] * scale_two[..., None],
    )


D_MODEL = 1536
HALF = 768
SLOTS = 32
OWN_SLOT = 12
SLAB = 8
MESH = pl.DeviceIdType.MESH


def moe_kernel(hid_ref, routes_ref, weight_ref, wgu_hbm, wdn_hbm, out_ref, wgu, wdn, send, recv, pair_send,
               pair_recv, back_send, back_recv, fin_send, fin_recv, load_sem, out_sem, in_sem, swap_sem):
    blk = lax.axis_index("blk")
    exp = lax.axis_index("expert")
    tp = lax.axis_index("tp")
    z = (blk // 4) * 8 + exp // 4
    y = blk % 4
    x = exp % 4

    def plane(dz, dx):
        zz = (z + dz + 16) % 16
        return ((zz // 8) * 4 + y, (zz % 8) * 4 + (x + dx) % 4, tp)

    sibling = (blk, exp, 1 - tp)
    loads = [
        pltpu.make_async_copy(wgu_hbm, wgu, load_sem.at[0]),
        pltpu.make_async_copy(wdn_hbm, wdn, load_sem.at[1]),
    ]
    for load in loads:
        load.start()

    barrier = pltpu.get_barrier_semaphore()

    def greet(i, carry):
        q = i + (i + 20) // 36
        pl.semaphore_signal(barrier, inc=1, device_id=plane(q // 4 - 4, q % 4), device_id_type=MESH)
        return carry

    lax.fori_loop(0, 35, greet, 0)
    pl.semaphore_signal(barrier, inc=1, device_id=sibling, device_id_type=MESH)

    rows = hid_ref.shape[0]
    mine = pl.ds(pl.multiple_of(tp * HALF, HALF), HALF)
    theirs = pl.ds(pl.multiple_of((1 - tp) * HALF, HALF), HALF)
    slot = lax.broadcasted_iota(jnp.int32, (SLOTS * SLAB, rows), 0)
    kk = slot // SLAB
    cc = slot % SLAB
    expert_of = ((exp // 4 + kk // 4 + 5) % 8) * 4 + (x + kk % 4) % 4
    named = jnp.zeros((SLOTS * SLAB, rows), jnp.float32)
    weighed = jnp.zeros((SLOTS * SLAB, rows), jnp.float32)
    for t in range(8):
        hit = expert_of == routes_ref[t : t + 1, :]
        named = named + jnp.where(hit, 1.0, 0.0)
        weighed = weighed + jnp.where(hit, weight_ref[t : t + 1, :], 0.0)
    earlier = jnp.where(
        lax.broadcasted_iota(jnp.int32, (rows, rows), 0) < lax.broadcasted_iota(jnp.int32, (rows, rows), 1), 1.0, 0.0
    ).astype(jnp.bfloat16)
    rank = jnp.dot(named.astype(jnp.bfloat16), earlier, preferred_element_type=jnp.float32)
    chosen = jnp.where((named > 0.5) & (jnp.abs(rank - cc.astype(jnp.float32)) < 0.5), 1.0, 0.0)
    weighed = weighed * chosen
    packed = jnp.dot(chosen.astype(jnp.bfloat16), hid_ref[:, mine], preferred_element_type=jnp.float32)
    send[...] = packed.astype(jnp.bfloat16).reshape(SLOTS, SLAB, HALF)
    recv[tp, OWN_SLOT] = packed[OWN_SLOT * SLAB : (OWN_SLOT + 1) * SLAB].astype(jnp.bfloat16)
    pl.semaphore_wait(barrier, 36)

    def ship(i, carry):
        k = i + (i + 20) // 32
        pltpu.make_async_remote_copy(
            src_ref=send.at[k], dst_ref=recv.at[tp, k], send_sem=out_sem.at[0], recv_sem=in_sem.at[0],
            device_id=plane(k // 4 - 3, k % 4), device_id_type=MESH,
        ).start()
        return carry

    lax.fori_loop(0, 31, ship, 0)
    pltpu.make_async_remote_copy(
        src_ref=send.at[pl.ds(0, 31)], dst_ref=recv.at[tp, pl.ds(0, 31)], send_sem=out_sem.at[0],
        recv_sem=in_sem.at[0], device_id=sibling, device_id_type=MESH,
    ).wait()
    swap = pltpu.make_async_remote_copy(
        src_ref=recv.at[tp], dst_ref=recv.at[tp], send_sem=swap_sem.at[0], recv_sem=swap_sem.at[1],
        device_id=sibling, device_id_type=MESH,
    )
    swap.start()
    for load in loads:
        load.wait()
    swap.wait()

    low = recv[0].reshape(SLOTS * SLAB, HALF)
    high = recv[1].reshape(SLOTS * SLAB, HALF)

    def proj(g):
        return jnp.dot(low, wgu[g, :HALF, :], preferred_element_type=jnp.float32) + jnp.dot(
            high, wgu[g, HALF:, :], preferred_element_type=jnp.float32
        )

    gate = proj(0)
    up = proj(1)
    hidden = (gate / (1.0 + jnp.exp(-gate)) * up).astype(jnp.bfloat16)
    pair_send[...] = jnp.dot(hidden, wdn[:, theirs], preferred_element_type=jnp.float32).astype(jnp.bfloat16)
    pair = pltpu.make_async_remote_copy(
        src_ref=pair_send, dst_ref=pair_recv, send_sem=swap_sem.at[2], recv_sem=swap_sem.at[3],
        device_id=sibling, device_id_type=MESH,
    )
    pair.start()
    part = jnp.dot(hidden, wdn[:, mine], preferred_element_type=jnp.float32)
    pair.wait()
    total = (part + pair_recv[...].astype(jnp.float32)).astype(jnp.bfloat16)
    back_send[...] = total.reshape(SLOTS, SLAB, HALF)
    back_recv[OWN_SLOT] = total[OWN_SLOT * SLAB : (OWN_SLOT + 1) * SLAB]

    def home(i, carry):
        k = i + (i + 20) // 32
        pltpu.make_async_remote_copy(
            src_ref=back_send.at[k], dst_ref=back_recv.at[k], send_sem=out_sem.at[1], recv_sem=in_sem.at[1],
            device_id=plane(3 - k // 4, 4 - k % 4), device_id_type=MESH,
        ).start()
        return carry

    lax.fori_loop(0, 31, home, 0)
    pltpu.make_async_remote_copy(
        src_ref=back_send.at[pl.ds(0, 31)], dst_ref=back_recv.at[pl.ds(0, 31)], send_sem=out_sem.at[1],
        recv_sem=in_sem.at[1], device_id=sibling, device_id_type=MESH,
    ).wait()
    got = back_recv[...].reshape(SLOTS * SLAB, HALF)
    w_high = weighed.astype(jnp.bfloat16)
    w_low = (weighed - w_high.astype(jnp.float32)).astype(jnp.bfloat16)
    dims = (((0,), (0,)), ((), ()))
    mixed = lax.dot_general(w_high, got, dims, preferred_element_type=jnp.float32) + lax.dot_general(
        w_low, got, dims, preferred_element_type=jnp.float32
    )
    fin_send[...] = mixed.astype(jnp.bfloat16)
    last = pltpu.make_async_remote_copy(
        src_ref=fin_send, dst_ref=fin_recv, send_sem=swap_sem.at[4], recv_sem=swap_sem.at[5],
        device_id=sibling, device_id_type=MESH,
    )
    last.start()
    out_ref[:, mine] = mixed.astype(jnp.bfloat16)
    last.wait()
    out_ref[:, theirs] = fin_recv[...]


def moe(hidden_in, routes, route_weight, w_gateup, w_down):
    bf = jnp.bfloat16
    vmem = pl.BlockSpec(memory_space=pltpu.VMEM)
    hbm = pl.BlockSpec(memory_space=pl.ANY)
    return pl.pallas_call(
        moe_kernel,
        out_shape=jax.ShapeDtypeStruct(hidden_in.shape, bf),
        in_specs=[vmem, vmem, vmem, hbm, hbm],
        out_specs=vmem,
        scratch_shapes=[
            pltpu.VMEM((2, D_MODEL, 256), bf),
            pltpu.VMEM((256, D_MODEL), bf),
            pltpu.VMEM((SLOTS, SLAB, HALF), bf),
            pltpu.VMEM((2, SLOTS, SLAB, HALF), bf),
            pltpu.VMEM((SLOTS * SLAB, HALF), bf),
            pltpu.VMEM((SLOTS * SLAB, HALF), bf),
            pltpu.VMEM((SLOTS, SLAB, HALF), bf),
            pltpu.VMEM((SLOTS, SLAB, HALF), bf),
            pltpu.VMEM((16, HALF), bf),
            pltpu.VMEM((16, HALF), bf),
            pltpu.SemaphoreType.DMA((2,)),
            pltpu.SemaphoreType.DMA((2,)),
            pltpu.SemaphoreType.DMA((2,)),
            pltpu.SemaphoreType.DMA((6,)),
        ],
        compiler_params=pltpu.CompilerParams(
            collective_id=1, has_side_effects=True, vmem_limit_bytes=40 * 1024 * 1024
        ),
    )(hidden_in, routes.T, route_weight.T, w_gateup[0].transpose(1, 0, 2), w_down[0])


def local(
    tokens,
    w_query,
    w_key,
    w_value,
    w_out,
    cache_keys,
    cache_values,
    parents,
    lengths,
    accepted_leaf,
    routes,
    route_weight,
    w_gateup,
    w_down,
):
    row_count = tokens.shape[0]
    model_width = tokens.shape[1]
    blk_count = lax.axis_size("blk")
    blk_rank = lax.axis_index("blk")
    req_count = parents.shape[0]
    tree_size = parents.shape[1]
    part_size = row_count // req_count
    head_size = HD
    head_count = w_query.shape[1] // head_size
    kv_count = w_key.shape[1] // head_size
    group_size = head_count // kv_count
    block_len = cache_keys.shape[1]
    kv_cols = kv_count * head_size
    reached = ancestry(parents)
    depths = (jnp.sum(reached, -1) - 1.0).astype(jnp.int32)
    slot_start = blk_rank * part_size
    own_depths = lax.dynamic_slice_in_dim(depths, slot_start, part_size, 1)
    positions = (lengths[:, None] + own_depths).reshape(-1)
    normed = rms_norm(tokens)
    query_raw = jnp.dot(
        normed,
        lax.all_gather(w_query, "expert", axis=0, tiled=True),
        preferred_element_type=jnp.float32,
    )
    key_raw = jnp.dot(
        normed,
        lax.all_gather(w_key, "expert", axis=0, tiled=True),
        preferred_element_type=jnp.float32,
    )
    value_raw = jnp.dot(
        normed,
        lax.all_gather(w_value, "expert", axis=0, tiled=True),
        preferred_element_type=jnp.float32,
    )
    own_queries = rotary(query_raw.reshape(row_count, head_count, head_size), positions).astype(
        jnp.bfloat16
    )
    key_rows = rotary(key_raw.reshape(row_count, kv_count, head_size), positions).astype(
        jnp.bfloat16
    )
    value_rows = value_raw.astype(jnp.bfloat16)
    tree_keys, tree_values = (
        lax.all_gather(key_rows.reshape(req_count, part_size, kv_cols), "blk", axis=1, tiled=True),
        lax.all_gather(
            value_rows.reshape(req_count, part_size, kv_cols), "blk", axis=1, tiled=True
        ),
    )
    own_query = own_queries.reshape(req_count, part_size, kv_count, group_size, head_size)
    own_reach = lax.dynamic_slice_in_dim(reached, slot_start, part_size, 1)
    running = attend_block(
        own_query,
        tree_keys.reshape(req_count, tree_size, kv_count, head_size),
        tree_values.reshape(req_count, tree_size, kv_count, head_size),
        (own_reach > 0.5)[:, :, None, None, :],
    )
    moving_keys = cache_keys
    moving_values = cache_values
    for turn_index in range(blk_count):
        source = (blk_rank - turn_index) % blk_count
        cache_pos = source * block_len + jnp.arange(block_len, dtype=jnp.int32)
        usable = (cache_pos[None, :] < lengths[:, None])[:, None, None, None, :]
        outcome = attend_block(
            own_query,
            moving_keys.reshape(req_count, block_len, kv_count, head_size),
            moving_values.reshape(req_count, block_len, kv_count, head_size),
            usable,
        )
        running = combine_parts(running, outcome)
        if turn_index + 1 < blk_count:
            moving_keys, moving_values = passed_along((moving_keys, moving_values), "blk", 1)
    context = (
        (running[2] / running[1][..., None])
        .reshape(row_count, head_count * head_size)
        .astype(jnp.bfloat16)
    )
    head_terms = jnp.dot(
        context,
        lax.all_gather(w_out, "expert", axis=1, tiled=True),
        preferred_element_type=jnp.float32,
    )
    attended = lax.psum(head_terms.astype(jnp.bfloat16), "tp")
    hidden_in = rms_norm(tokens.astype(jnp.float32) + residual_scale * attended.astype(jnp.float32))
    expert_mix = moe(hidden_in, routes, route_weight, w_gateup, w_down)
    leaf_pick = (jnp.arange(tree_size, dtype=jnp.int32)[None, :] == accepted_leaf[:, None]).astype(
        jnp.float32
    )
    path_mask = jnp.sum(leaf_pick[:, :, None] * reached, 1)
    target_pos = lengths[:, None] + depths
    block_pos = blk_rank * block_len + jnp.arange(block_len, dtype=jnp.int32)
    placing_mask = (block_pos[None, :, None] == target_pos[:, None, :]) & (
        path_mask[:, None, :] > 0.5
    )
    written = jnp.any(placing_mask, -1)
    placing = placing_mask.astype(jnp.bfloat16)
    moved_keys = jnp.einsum(
        "rpt,rtc->rpc", placing, tree_keys, preferred_element_type=jnp.float32
    ).astype(jnp.bfloat16)
    moved_values = jnp.einsum(
        "rpt,rtc->rpc", placing, tree_values, preferred_element_type=jnp.float32
    ).astype(jnp.bfloat16)
    new_keys = jnp.where(written[:, :, None], moved_keys, cache_keys)
    new_values = jnp.where(written[:, :, None], moved_values, cache_values)
    return (attended, expert_mix, new_keys, new_values)


def solution(mesh):
    in_specs = (
        P(("blk", "expert"), None),
        P("expert", "tp"),
        P("expert", "tp"),
        P("expert", "tp"),
        P("tp", "expert"),
        P("expert", "blk", "tp"),
        P("expert", "blk", "tp"),
        P("expert", None),
        P("expert"),
        P("expert"),
        P(("blk", "expert"), None),
        P(("blk", "expert"), None),
        P("expert", None, None, "tp"),
        P("expert", "tp", None),
    )
    out_specs = (
        P(("blk", "expert"), None),
        P(("blk", "expert"), None),
        P("expert", "blk", "tp"),
        P("expert", "blk", "tp"),
    )
    return jax.shard_map(local, mesh=mesh, in_specs=in_specs, out_specs=out_specs, check_vma=False)
```

```python
import jax
import jax.numpy as jnp
from jax import lax
from jax.experimental import pallas as pl
from jax.experimental.pallas import tpu as pltpu
from jax.sharding import PartitionSpec as P

score_scale = 0.015625
residual_scale = 0.22
masked_score = -1e30
D_MODEL = 1536
HALF = 768
SLOTS = 32
OWN_SLOT = 12
SLAB = 8
MESH = pl.DeviceIdType.MESH


def moe_kernel(hid_ref, routes_ref, weight_ref, wgu_hbm, wdn_hbm, out_ref, wgu, wdn, send, recv, pair_send,
               pair_recv, back_send, back_recv, fin_send, fin_recv, load_sem, out_sem, in_sem, swap_sem):
    blk = lax.axis_index("blk")
    exp = lax.axis_index("expert")
    tp = lax.axis_index("tp")
    z = (blk // 4) * 8 + exp // 4
    y = blk % 4
    x = exp % 4

    def plane(dz, dx):
        zz = (z + dz + 16) % 16
        return ((zz // 8) * 4 + y, (zz % 8) * 4 + (x + dx) % 4, tp)

    sibling = (blk, exp, 1 - tp)
    loads = [
        pltpu.make_async_copy(wgu_hbm, wgu, load_sem.at[0]),
        pltpu.make_async_copy(wdn_hbm, wdn, load_sem.at[1]),
    ]
    for load in loads:
        load.start()

    barrier = pltpu.get_barrier_semaphore()

    def greet(i, carry):
        q = i + (i + 20) // 36
        pl.semaphore_signal(barrier, inc=1, device_id=plane(q // 4 - 4, q % 4), device_id_type=MESH)
        return carry

    lax.fori_loop(0, 35, greet, 0)
    pl.semaphore_signal(barrier, inc=1, device_id=sibling, device_id_type=MESH)

    rows = hid_ref.shape[0]
    mine = pl.ds(pl.multiple_of(tp * HALF, HALF), HALF)
    theirs = pl.ds(pl.multiple_of((1 - tp) * HALF, HALF), HALF)
    slot = lax.broadcasted_iota(jnp.int32, (SLOTS * SLAB, rows), 0)
    kk = slot // SLAB
    cc = slot % SLAB
    expert_of = ((exp // 4 + kk // 4 + 5) % 8) * 4 + (x + kk % 4) % 4
    named = jnp.zeros((SLOTS * SLAB, rows), jnp.float32)
    weighed = jnp.zeros((SLOTS * SLAB, rows), jnp.float32)
    for t in range(8):
        hit = expert_of == routes_ref[t : t + 1, :]
        named = named + jnp.where(hit, 1.0, 0.0)
        weighed = weighed + jnp.where(hit, weight_ref[t : t + 1, :], 0.0)
    earlier = jnp.where(
        lax.broadcasted_iota(jnp.int32, (rows, rows), 0) < lax.broadcasted_iota(jnp.int32, (rows, rows), 1), 1.0, 0.0
    ).astype(jnp.bfloat16)
    rank = jnp.dot(named.astype(jnp.bfloat16), earlier, preferred_element_type=jnp.float32)
    chosen = jnp.where((named > 0.5) & (jnp.abs(rank - cc.astype(jnp.float32)) < 0.5), 1.0, 0.0)
    weighed = weighed * chosen
    packed = jnp.dot(chosen.astype(jnp.bfloat16), hid_ref[:, mine], preferred_element_type=jnp.float32)
    send[...] = packed.astype(jnp.bfloat16).reshape(SLOTS, SLAB, HALF)
    recv[tp, OWN_SLOT] = packed[OWN_SLOT * SLAB : (OWN_SLOT + 1) * SLAB].astype(jnp.bfloat16)
    pl.semaphore_wait(barrier, 36)

    def ship(i, carry):
        k = i + (i + 20) // 32
        pltpu.make_async_remote_copy(
            src_ref=send.at[k], dst_ref=recv.at[tp, k], send_sem=out_sem.at[0], recv_sem=in_sem.at[0],
            device_id=plane(k // 4 - 3, k % 4), device_id_type=MESH,
        ).start()
        return carry

    lax.fori_loop(0, 31, ship, 0)
    pltpu.make_async_remote_copy(
        src_ref=send.at[pl.ds(0, 31)], dst_ref=recv.at[tp, pl.ds(0, 31)], send_sem=out_sem.at[0],
        recv_sem=in_sem.at[0], device_id=sibling, device_id_type=MESH,
    ).wait()
    swap = pltpu.make_async_remote_copy(
        src_ref=recv.at[tp], dst_ref=recv.at[tp], send_sem=swap_sem.at[0], recv_sem=swap_sem.at[1],
        device_id=sibling, device_id_type=MESH,
    )
    swap.start()
    for load in loads:
        load.wait()
    swap.wait()

    low = recv[0].reshape(SLOTS * SLAB, HALF)
    high = recv[1].reshape(SLOTS * SLAB, HALF)

    def proj(g):
        return jnp.dot(low, wgu[g, :HALF, :], preferred_element_type=jnp.float32) + jnp.dot(
            high, wgu[g, HALF:, :], preferred_element_type=jnp.float32
        )

    gate = proj(0)
    up = proj(1)
    hidden = (gate / (1.0 + jnp.exp(-gate)) * up).astype(jnp.bfloat16)
    pair_send[...] = jnp.dot(hidden, wdn[:, theirs], preferred_element_type=jnp.float32).astype(jnp.bfloat16)
    pair = pltpu.make_async_remote_copy(
        src_ref=pair_send, dst_ref=pair_recv, send_sem=swap_sem.at[2], recv_sem=swap_sem.at[3],
        device_id=sibling, device_id_type=MESH,
    )
    pair.start()
    part = jnp.dot(hidden, wdn[:, mine], preferred_element_type=jnp.float32)
    pair.wait()
    total = (part + pair_recv[...].astype(jnp.float32)).astype(jnp.bfloat16)
    back_send[...] = total.reshape(SLOTS, SLAB, HALF)
    back_recv[OWN_SLOT] = total[OWN_SLOT * SLAB : (OWN_SLOT + 1) * SLAB]

    def home(i, carry):
        k = i + (i + 20) // 32
        pltpu.make_async_remote_copy(
            src_ref=back_send.at[k], dst_ref=back_recv.at[k], send_sem=out_sem.at[1], recv_sem=in_sem.at[1],
            device_id=plane(3 - k // 4, 4 - k % 4), device_id_type=MESH,
        ).start()
        return carry

    lax.fori_loop(0, 31, home, 0)
    pltpu.make_async_remote_copy(
        src_ref=back_send.at[pl.ds(0, 31)], dst_ref=back_recv.at[pl.ds(0, 31)], send_sem=out_sem.at[1],
        recv_sem=in_sem.at[1], device_id=sibling, device_id_type=MESH,
    ).wait()
    got = back_recv[...].reshape(SLOTS * SLAB, HALF)
    w_high = weighed.astype(jnp.bfloat16)
    w_low = (weighed - w_high.astype(jnp.float32)).astype(jnp.bfloat16)
    dims = (((0,), (0,)), ((), ()))
    mixed = lax.dot_general(w_high, got, dims, preferred_element_type=jnp.float32) + lax.dot_general(
        w_low, got, dims, preferred_element_type=jnp.float32
    )
    fin_send[...] = mixed.astype(jnp.bfloat16)
    last = pltpu.make_async_remote_copy(
        src_ref=fin_send, dst_ref=fin_recv, send_sem=swap_sem.at[4], recv_sem=swap_sem.at[5],
        device_id=sibling, device_id_type=MESH,
    )
    last.start()
    out_ref[:, mine] = mixed.astype(jnp.bfloat16)
    last.wait()
    out_ref[:, theirs] = fin_recv[...]


def moe(hidden_in, routes, route_weight, w_gateup, w_down):
    bf = jnp.bfloat16
    vmem = pl.BlockSpec(memory_space=pltpu.VMEM)
    hbm = pl.BlockSpec(memory_space=pl.ANY)
    return pl.pallas_call(
        moe_kernel,
        out_shape=jax.ShapeDtypeStruct(hidden_in.shape, bf),
        in_specs=[vmem, vmem, vmem, hbm, hbm],
        out_specs=vmem,
        scratch_shapes=[
            pltpu.VMEM((2, D_MODEL, 256), bf),
            pltpu.VMEM((256, D_MODEL), bf),
            pltpu.VMEM((SLOTS, SLAB, HALF), bf),
            pltpu.VMEM((2, SLOTS, SLAB, HALF), bf),
            pltpu.VMEM((SLOTS * SLAB, HALF), bf),
            pltpu.VMEM((SLOTS * SLAB, HALF), bf),
            pltpu.VMEM((SLOTS, SLAB, HALF), bf),
            pltpu.VMEM((SLOTS, SLAB, HALF), bf),
            pltpu.VMEM((16, HALF), bf),
            pltpu.VMEM((16, HALF), bf),
            pltpu.SemaphoreType.DMA((2,)),
            pltpu.SemaphoreType.DMA((2,)),
            pltpu.SemaphoreType.DMA((2,)),
            pltpu.SemaphoreType.DMA((6,)),
        ],
        compiler_params=pltpu.CompilerParams(
            collective_id=1, has_side_effects=True, vmem_limit_bytes=40 * 1024 * 1024
        ),
    )(hidden_in, routes.T, route_weight.T, w_gateup[0].transpose(1, 0, 2), w_down[0])


TREE = 64
ROWS = 128
CARRIED = 160


def attend_kernel(len_ref, leaf_ref, tok_ref, wq_ref, wk_ref, wv_ref, ck_ref, cv_ref, par_ref, wo_hbm, att_ref, hid_ref,
                  nk_ref, nv_ref, toks, slices, wall, wout, normed_ref, made, part_send, part_recv, stat_send, stat_recv,
                  pair_send, pair_recv, tok_out, tok_in, made_out, made_in, qa_out, qa_in, qb_out, qb_in, oa_out, oa_in,
                  ob_out, ob_in, part_sem, pair_sem, own_sem):
    f32, bf = jnp.float32, jnp.bfloat16
    blk = lax.axis_index("blk")
    exp = lax.axis_index("expert")
    tp = lax.axis_index("tp")
    hi = blk // 4
    y = blk % 4
    z = hi * 8 + exp // 4
    x = exp % 4
    partner = (1 - hi) * 4 + y

    def along_z(dz):
        zz = (z + dz + 16) % 16
        return ((zz // 8) * 4 + y, (zz % 8) * 4 + x, tp)

    def along_x(dx):
        return (blk, (exp // 4) * 4 + (x + dx) % 4, tp)

    def along_y(dy):
        return (hi * 4 + (y + dy) % 4, exp, tp)

    across = (partner, exp, tp)
    sibling = (blk, exp, 1 - tp)

    def source_row(slot):
        return ((z - (slot - 3) + 16) % 8) * 4 + x

    def remote(src, dst, ssem, rsem, device):
        return pltpu.make_async_remote_copy(
            src_ref=src, dst_ref=dst, send_sem=ssem, recv_sem=rsem, device_id=device, device_id_type=MESH
        )

    own_out = pltpu.make_async_copy(wo_hbm, wout.at[exp], own_sem.at[0])
    own_out.start()

    barrier = pltpu.get_barrier_semaphore()

    def greet_z(i, carry):
        pl.semaphore_signal(barrier, inc=1, device_id=along_z(i - 4 + (i + 4) // 8), device_id_type=MESH)
        return carry

    lax.fori_loop(0, 8, greet_z, 0)
    for d in range(1, 4):
        pl.semaphore_signal(barrier, inc=1, device_id=along_x(d), device_id_type=MESH)

    def greet_blk(i, carry):
        pl.semaphore_signal(barrier, inc=1, device_id=((blk + 1 + i) % 8, exp, tp), device_id_type=MESH)
        return carry

    lax.fori_loop(0, 7, greet_blk, 0)
    pl.semaphore_signal(barrier, inc=1, device_id=sibling, device_id_type=MESH)

    for b in range(8):
        if b < 6:
            slices[b, :, 0:128] = wq_ref[:, b * 128 : (b + 1) * 128]
        else:
            slices[b, :, 0:128] = wk_ref[:, (b - 6) * 128 : (b - 5) * 128]
        slices[b, :, 128:256] = wv_ref[:, (b // 4) * 128 : (b // 4 + 1) * 128]
    wall[exp] = slices[blk]
    toks[blk] = tok_ref[...]
    pl.semaphore_wait(barrier, 19)

    def share_start(buf, ssem, rsem):
        for d in range(1, 4):
            remote(buf.at[blk], buf.at[blk], ssem.at[d - 1], rsem.at[d - 1], along_y(d)).start()
        remote(buf.at[blk], buf.at[blk], ssem.at[3], rsem.at[3], across).start()

    def share_forward(buf, ssem, rsem):
        remote(buf.at[partner], buf.at[partner], ssem.at[3], rsem.at[3], across).wait_recv()
        for d in range(1, 4):
            remote(buf.at[partner], buf.at[partner], ssem.at[3 + d], rsem.at[3 + d], along_y(d)).start()

    def share_finish(buf, ssem, rsem):
        for d in range(1, 4):
            for half in range(2):
                remote(
                    buf.at[blk], buf.at[(hi + half) % 2 * 4 + (y + 4 - d) % 4], ssem.at[d - 1 + 4 * half],
                    rsem.at[d - 1 + 4 * half], across,
                ).wait_recv()

    def share_sent(buf, ssem, rsem):
        for s in range(7):
            remote(buf.at[blk], buf.at[blk], ssem.at[s], rsem.at[s], across).wait_send()

    def slot_of(i):
        return i + (i + 5) // 8

    share_start(toks, tok_out, tok_in)

    def weights_a(i, carry):
        slot = slot_of(i)
        to = along_z(slot - 3)
        remote(slices.at[to[0]], wall.at[exp], qa_out.at[0], qa_in.at[slot], to).start()
        return carry

    lax.fori_loop(0, 7, weights_a, 0)

    def pass_on(slot, buf, ssem, rsem):
        row = source_row(slot)
        for d in range(1, 4):
            remote(buf.at[row], buf.at[row], ssem.at[0], rsem.at[0], along_x(d)).start()

    pass_on(3, wall, qb_out, qb_in)

    def out_a(i, carry):
        slot = slot_of(i)
        remote(wo_hbm, wout.at[exp], oa_out.at[0], oa_in.at[slot], along_z(slot - 3)).start()
        return carry

    lax.fori_loop(0, 7, out_a, 0)

    lane = lax.broadcasted_iota(jnp.int32, (ROWS, 128), 1)
    line = lax.broadcasted_iota(jnp.int32, (ROWS, 128), 0)
    parent = par_ref[...]
    parent = jnp.where(parent >= 0, parent + 64 * (lax.broadcasted_iota(jnp.int32, (1, 128), 1) // 64), -1)
    eye = jnp.where(lane == line, 1.0, 0.0)
    upward = eye + jnp.where(line == parent, 1.0, 0.0)
    for doubling in range(6):
        short = upward.astype(bf)
        upward = jnp.minimum(upward + jnp.dot(short, short, preferred_element_type=f32), 1.0)
    upward_bf = upward.astype(bf)
    dims0 = (((0,), (0,)), ((), ()))
    reach = lax.dot_general(upward_bf, eye.astype(bf), dims0, preferred_element_type=f32)
    depth = lax.dot_general(upward_bf, jnp.ones((ROWS, 128), bf), dims0, preferred_element_type=f32) - 1.0
    len0 = len_ref[0].astype(f32)
    len1 = len_ref[1].astype(f32)
    place = depth + jnp.where(line < 64, len0, len1)
    rate = jnp.exp((lane % 32).astype(f32) * (-9.210340371976184 / 32.0))
    angle = place * rate
    cos = jnp.cos(angle)
    low_half = (lane % 64) < 32
    sin = jnp.where(low_half, -1.0, 1.0) * jnp.sin(angle)
    target = jnp.sum(upward, axis=0, keepdims=True) - 1.0 + jnp.where(lane[0:1] < 64, len0, len1)
    on_path = jnp.sum(
        jnp.where((line == leaf_ref[0]) | (line == leaf_ref[1] + 64), reach, 0.0), axis=0, keepdims=True
    )

    share_forward(toks, tok_out, tok_in)

    def weights_b(i, carry):
        slot = slot_of(i)
        row = source_row(slot)
        remote(wall.at[row], wall.at[row], qa_out.at[0], qa_in.at[slot], across).wait_recv()
        pass_on(slot, wall, qb_out, qb_in)
        return carry

    lax.fori_loop(0, 7, weights_b, 0)
    share_finish(toks, tok_out, tok_in)

    for r in range(2):
        rows = toks[:, r].reshape(TREE, D_MODEL).astype(f32)
        scale = lax.rsqrt(jnp.mean(rows * rows, axis=-1, keepdims=True) + 1e-06)
        normed_ref[r * TREE : (r + 1) * TREE, :] = (rows * scale).astype(bf)
    remote(wall.at[pl.ds(0, 24)], wall.at[pl.ds(0, 24)], qb_out.at[0], qb_in.at[0], across).wait_recv()
    w_first = wall[:, :, 0:128].reshape(D_MODEL, 128)
    w_second = wall[:, :, 128:256].reshape(D_MODEL, 128)
    first = jnp.dot(normed_ref[...], w_first, preferred_element_type=f32)
    turned = jnp.where(low_half, pltpu.roll(first, 96, 1), pltpu.roll(first, 32, 1))
    made[blk, 0:ROWS, :] = (first * cos + turned * sin).astype(bf)
    quarter = normed_ref[pl.ds(pl.multiple_of(y * 32, 32), 32), :]
    made[blk, ROWS:CARRIED, :] = jnp.dot(quarter, w_second, preferred_element_type=f32).astype(bf)

    share_start(made, made_out, made_in)

    own_out.wait()
    pass_on(3, wout, ob_out, ob_in)

    def out_b(i, carry):
        slot = slot_of(i)
        row = source_row(slot)
        remote(wout.at[row], wout.at[row], oa_out.at[0], oa_in.at[slot], across).wait_recv()
        pass_on(slot, wout, ob_out, ob_in)
        return carry

    share_forward(made, made_out, made_in)
    lax.fori_loop(0, 7, out_b, 0)
    share_finish(made, made_out, made_in)

    tree_k = [made[6 + c, 0:ROWS, :] for c in range(2)]
    tree_v = [jnp.concatenate([made[c * 4 + q, ROWS:CARRIED, :] for q in range(4)], axis=0) for c in range(2)]
    nt = (((1,), (1,)), ((), ()))
    left = lane < 64
    for r in range(2):
        length = len0 if r == 0 else len1
        sees = (lane[0:1] + blk * 128).astype(f32) < length
        tree_ok = (reach[r * TREE : (r + 1) * TREE] > 0.5) & (((lane[0:TREE] % 64) // 8) == blk)
        left64 = left[0:TREE]
        lane64 = lane[0:TREE]
        stat = jnp.zeros((TREE, 128), f32)
        tops = []
        for c in range(2):
            stack = []
            for head in range(6 * c, 6 * c + 6):
                block = made[head // 2, r * TREE : (r + 1) * TREE, :].astype(f32)
                side = (head // 3) % 2
                if side != head % 2:
                    block = pltpu.roll(block, 64, 1)
                stack.append(jnp.where(left64 if side == 0 else ~left64, block, 0.0).astype(bf))
            query = jnp.concatenate(stack, axis=0)
            cols = slice(c * 128, (c + 1) * 128)
            s_cache = lax.dot_general(query, ck_ref[r, :, cols], nt, preferred_element_type=f32) * score_scale
            s_tree = lax.dot_general(query, tree_k[c], nt, preferred_element_type=f32) * score_scale
            s_cache = jnp.where(sees, s_cache, masked_score).reshape(6, TREE, 128)
            s_tree = jnp.where(tree_ok, s_tree.reshape(6, TREE, 128), masked_score)
            peak = jnp.maximum(
                jnp.max(s_cache, axis=-1, keepdims=True), jnp.max(s_tree, axis=-1, keepdims=True)
            )
            p_cache = jnp.where(sees, jnp.exp(s_cache - peak), 0.0)
            p_tree = jnp.where(tree_ok, jnp.exp(s_tree - peak), 0.0)
            mass = jnp.sum(p_cache, axis=-1, keepdims=True) + jnp.sum(p_tree, axis=-1, keepdims=True)
            total = jnp.dot(
                p_cache.reshape(6 * TREE, 128).astype(bf), cv_ref[r, :, cols], preferred_element_type=f32
            ) + jnp.dot(p_tree.reshape(6 * TREE, 128).astype(bf), tree_v[c], preferred_element_type=f32)
            total = total.reshape(6, TREE, 128) / jnp.where(mass > 0.0, mass, 1.0)
            for n in range(6):
                head = 6 * c + n
                stat = jnp.where(lane64 == head, peak[n], stat)
                stat = jnp.where(lane64 == 64 + head, mass[n], stat)
                tops.append(total[n])
        for i in range(6):
            parts = []
            for u in range(2):
                head = 2 * i + u
                value = tops[head]
                if (head // 3) % 2 != u:
                    value = pltpu.roll(value, 64, 1)
                parts.append(value)
            joined = jnp.where(left64, parts[0], parts[1])
            part_send[:, r, :, i * 128 : (i + 1) * 128] = joined.astype(bf).reshape(8, 8, 128)
        stat_send[:, r, :, :] = stat.reshape(8, 8, 128)

    def parts_out(i, carry):
        to = (blk + 1 + i) % 8
        remote(part_send.at[to], part_recv.at[blk], part_sem.at[0], part_sem.at[1], (to, exp, tp)).start()
        remote(stat_send.at[to], stat_recv.at[blk], part_sem.at[2], part_sem.at[3], (to, exp, tp)).start()
        return carry

    lax.fori_loop(0, 7, parts_out, 0)
    part_recv[blk] = part_send[blk]
    stat_recv[blk] = stat_send[blk]

    for r in range(2):
        spot = (line + blk * 128).astype(f32)
        placing = jnp.where((spot == target) & (on_path > 0.5) & ((lane // 64) == r), 1.0, 0.0)
        written = jnp.max(placing, axis=-1, keepdims=True) > 0.5
        placing = placing.astype(bf)
        for c in range(2):
            cols = slice(c * 128, (c + 1) * 128)
            moved_k = jnp.dot(placing, tree_k[c], preferred_element_type=f32)
            nk_ref[r, :, cols] = jnp.where(written, moved_k, ck_ref[r, :, cols].astype(f32)).astype(bf)
            moved_v = jnp.dot(placing, tree_v[c], preferred_element_type=f32)
            nv_ref[r, :, cols] = jnp.where(written, moved_v, cv_ref[r, :, cols].astype(f32)).astype(bf)

    remote(part_send.at[pl.ds(0, 7)], part_recv.at[pl.ds(0, 7)], part_sem.at[0], part_sem.at[1], across).wait()
    remote(stat_send.at[pl.ds(0, 7)], stat_recv.at[pl.ds(0, 7)], part_sem.at[2], part_sem.at[3], across).wait()
    stats = stat_recv[...].reshape(8, 16, 128)
    masses = pltpu.roll(stats.reshape(ROWS, 128), 64, 1).reshape(8, 16, 128)
    peak = jnp.max(stats, axis=0, keepdims=True)
    share = jnp.where(lane[0:16] < 12, masses * jnp.exp(stats - peak), 0.0)
    whole = jnp.sum(share, axis=0, keepdims=True)
    share = (share / jnp.where(whole > 0.0, whole, 1.0)).reshape(ROWS, 128)
    spread = jnp.where(
        lax.broadcasted_iota(jnp.int32, (128, HALF), 1) // 64 == lax.broadcasted_iota(jnp.int32, (128, HALF), 0), 1.0, 0.0
    ).astype(bf)
    share_high = share.astype(bf)
    share_low = (share - share_high.astype(f32)).astype(bf)
    factor = jnp.dot(share_high, spread, preferred_element_type=f32) + jnp.dot(
        share_low, spread, preferred_element_type=f32
    )
    context = jnp.sum(
        factor.reshape(8, 16, HALF) * part_recv[...].reshape(8, 16, HALF).astype(f32), axis=0
    ).astype(bf)
    remote(wout.at[pl.ds(0, 24)], wout.at[pl.ds(0, 24)], ob_out.at[0], ob_in.at[0], across).wait_recv()
    terms = lax.dot_general(context, wout[...].reshape(D_MODEL, HALF), nt, preferred_element_type=f32).astype(bf)
    pair_send[...] = terms
    pair = remote(pair_send, pair_recv, pair_sem.at[0], pair_sem.at[1], sibling)
    pair.start()
    pair.wait()
    attended = (terms.astype(f32) + pair_recv[...].astype(f32)).astype(bf)
    att_ref[...] = attended
    mixed = tok_ref[...].reshape(16, D_MODEL).astype(f32) + residual_scale * attended.astype(f32)
    scale = lax.rsqrt(jnp.mean(mixed * mixed, axis=-1, keepdims=True) + 1e-06)
    hid_ref[...] = (mixed * scale).astype(bf)

    share_sent(toks, tok_out, tok_in)
    share_sent(made, made_out, made_in)
    remote(wall.at[pl.ds(0, 7)], wall.at[pl.ds(0, 7)], qa_out.at[0], qb_in.at[0], across).wait_send()
    remote(wall.at[pl.ds(0, 24)], wall.at[pl.ds(0, 24)], qb_out.at[0], qb_in.at[0], across).wait_send()
    remote(wout.at[pl.ds(0, 7)], wout.at[pl.ds(0, 7)], oa_out.at[0], ob_in.at[0], across).wait_send()
    remote(wout.at[pl.ds(0, 24)], wout.at[pl.ds(0, 24)], ob_out.at[0], ob_in.at[0], across).wait_send()


def attend(tokens, w_query, w_key, w_value, w_out, cache_keys, cache_values, parents, lengths, accepted_leaf):
    bf = jnp.bfloat16
    vmem = pl.BlockSpec(memory_space=pltpu.VMEM)
    smem = pl.BlockSpec(memory_space=pltpu.SMEM)
    dma = pltpu.SemaphoreType.DMA
    return pl.pallas_call(
        attend_kernel,
        out_shape=(
            jax.ShapeDtypeStruct(tokens.shape, bf),
            jax.ShapeDtypeStruct(tokens.shape, bf),
            jax.ShapeDtypeStruct(cache_keys.shape, bf),
            jax.ShapeDtypeStruct(cache_values.shape, bf),
        ),
        in_specs=[smem, smem] + [vmem] * 7 + [pl.BlockSpec(memory_space=pl.ANY)],
        out_specs=(vmem,) * 4,
        scratch_shapes=[
            pltpu.VMEM((8, 2, 8, D_MODEL), bf),
            pltpu.VMEM((8, 48, 256), bf),
            pltpu.VMEM((32, 48, 256), bf),
            pltpu.VMEM((32, 48, HALF), bf),
            pltpu.VMEM((ROWS, D_MODEL), bf),
            pltpu.VMEM((8, CARRIED, 128), bf),
            pltpu.VMEM((8, 2, 8, HALF), bf),
            pltpu.VMEM((8, 2, 8, HALF), bf),
            pltpu.VMEM((8, 2, 8, 128), jnp.float32),
            pltpu.VMEM((8, 2, 8, 128), jnp.float32),
            pltpu.VMEM((16, D_MODEL), bf),
            pltpu.VMEM((16, D_MODEL), bf),
            dma((7,)), dma((7,)), dma((7,)), dma((7,)),
            dma((1,)), dma((8,)), dma((1,)), dma((1,)),
            dma((1,)), dma((8,)), dma((1,)), dma((1,)),
            dma((4,)), dma((2,)), dma((1,)),
        ],
        compiler_params=pltpu.CompilerParams(
            collective_id=2, has_side_effects=True, vmem_limit_bytes=40 * 1024 * 1024
        ),
    )(
        lengths, accepted_leaf, tokens.reshape(2, 8, D_MODEL), w_query, w_key, w_value, cache_keys, cache_values,
        parents.reshape(1, 128), w_out.T,
    )


def local(tokens, w_query, w_key, w_value, w_out, cache_keys, cache_values, parents, lengths, accepted_leaf, routes,
          route_weight, w_gateup, w_down):
    attended, hidden_in, new_keys, new_values = attend(
        tokens, w_query, w_key, w_value, w_out, cache_keys, cache_values, parents, lengths, accepted_leaf
    )
    expert_mix = moe(hidden_in, routes, route_weight, w_gateup, w_down)
    return (attended, expert_mix, new_keys, new_values)


def solution(mesh):
    in_specs = (
        P(("blk", "expert"), None),
        P("expert", "tp"),
        P("expert", "tp"),
        P("expert", "tp"),
        P("tp", "expert"),
        P("expert", "blk", "tp"),
        P("expert", "blk", "tp"),
        P("expert", None),
        P("expert"),
        P("expert"),
        P(("blk", "expert"), None),
        P(("blk", "expert"), None),
        P("expert", None, None, "tp"),
        P("expert", "tp", None),
    )
    out_specs = (
        P(("blk", "expert"), None),
        P(("blk", "expert"), None),
        P("expert", "blk", "tp"),
        P("expert", "blk", "tp"),
    )
    return jax.shard_map(local, mesh=mesh, in_specs=in_specs, out_specs=out_specs, check_vma=False)
```

```python
import jax
import jax.numpy as jnp
from jax import lax
from jax.experimental import pallas as pl
from jax.experimental.pallas import tpu as pltpu
from jax.sharding import PartitionSpec as P

score_scale = 0.015625
residual_scale = 0.22
masked_score = -1e30
D_MODEL = 1536
HALF = 768
SLOTS = 32
OWN_SLOT = 12
SLAB = 8
TREE = 64
ROWS = 128
CARRIED = 160
MESH = pl.DeviceIdType.MESH


def layer_kernel(len_hbm, leaf_hbm, tok_hbm, wq_hbm, wk_hbm, wv_hbm, ck_hbm, cv_hbm, par_hbm, wo_hbm, routes_hbm, weight_hbm,
                 wgu_hbm, wdn_hbm, att_ref, mix_ref, nk_ref, nv_ref, len_ref, leaf_ref, tok_ref, wq_ref, wk_ref, wv_ref,
                 ck_ref, cv_ref, par_ref, routes_ref, weight_ref, wgu, wdn, toks, slices, wall, wout, normed_ref, made,
                 part_send, near_recv, stat_send, near_stat, far_send, far_recv, far_stat_send, far_stat, pair_send,
                 pair_recv, send, recv, half_send, half_recv, back_send, back_recv, fin_send, fin_recv, load_sem, tok_out,
                 tok_in, made_out, made_in, qa_out, qa_in, qb_out, qb_in, oa_out, oa_in, ob_out, ob_in, part_sem,
                 pair_sem, ship_out, ship_in):
    f32, bf = jnp.float32, jnp.bfloat16
    blk = lax.axis_index("blk")
    exp = lax.axis_index("expert")
    tp = lax.axis_index("tp")
    hi = lax.div(blk, 4)
    y = lax.rem(blk, 4)
    z_lo = lax.div(exp, 4)
    z = hi * 8 + z_lo
    x = lax.rem(exp, 4)
    partner = (1 - hi) * 4 + y
    z_blk, z_exp = {}, {}
    for dz in range(-4, 5):
        zz = lax.rem(z + (dz + 16), 16)
        z_blk[dz] = lax.div(zz, 8) * 4 + y
        z_exp[dz] = lax.rem(zz, 8) * 4
    x_at = {dx: lax.rem(x + dx, 4) for dx in range(4)}
    y_at = {dy: lax.rem(y + dy, 4) for dy in range(4)}

    def plane(dz, dx):
        return (z_blk[dz], z_exp[dz] + x_at[dx], tp)

    def along_z(dz):
        return plane(dz, 0)

    def along_x(dx):
        return plane(0, dx)

    def along_y(dy):
        return (hi * 4 + y_at[dy], exp, tp)

    across = (partner, exp, tp)
    sibling = (blk, exp, 1 - tp)

    def source_row(slot):
        return lax.rem(z_lo + (11 - slot), 8) * 4 + x

    def remote(src, dst, ssem, rsem, device):
        return pltpu.make_async_remote_copy(
            src_ref=src, dst_ref=dst, send_sem=ssem, recv_sem=rsem, device_id=device, device_id_type=MESH
        )

    pairs = (
        (wq_hbm, wq_ref), (wk_hbm, wk_ref), (wv_hbm, wv_ref), (tok_hbm, tok_ref), (len_hbm, len_ref),
        (leaf_hbm, leaf_ref), (par_hbm, par_ref), (routes_hbm, routes_ref), (weight_hbm, weight_ref), (ck_hbm, ck_ref),
        (cv_hbm, cv_ref), (wo_hbm, wout.at[exp]), (wgu_hbm, wgu), (wdn_hbm, wdn),
    )
    loads = [pltpu.make_async_copy(src, dst, load_sem.at[n]) for n, (src, dst) in enumerate(pairs)]
    for load in loads:
        load.start()

    barrier = pltpu.get_barrier_semaphore()

    def greet(device):
        pl.semaphore_signal(barrier, inc=1, device_id=device, device_id_type=MESH)

    for d in range(1, 8):
        greet((lax.rem(blk + d, 8), exp, tp))
    for dz in (-4, 4, -3, 3, -2, 2, -1, 1, 0):
        for dx in range(4):
            if dz or dx:
                greet(plane(dz, dx))
    greet(sibling)

    for n in range(4):
        loads[n].wait()
    for b in range(8):
        if b < 6:
            slices[b, :, 0:128] = wq_ref[:, b * 128 : (b + 1) * 128]
        else:
            slices[b, :, 0:128] = wk_ref[:, (b - 6) * 128 : (b - 5) * 128]
        slices[b, :, 128:256] = wv_ref[:, (b // 4) * 128 : (b // 4 + 1) * 128]
    wall[exp] = slices[blk]
    toks[blk] = tok_ref[...]
    pl.semaphore_wait(barrier, 43)

    def share_start(buf, ssem, rsem):
        remote(buf.at[blk], buf.at[blk], ssem.at[3], rsem.at[3], across).start()
        for d in range(1, 4):
            remote(buf.at[blk], buf.at[blk], ssem.at[d - 1], rsem.at[d - 1], along_y(d)).start()

    def share_forward(buf, ssem, rsem):
        remote(buf.at[partner], buf.at[partner], ssem.at[3], rsem.at[3], across).wait_recv()
        for d in range(1, 4):
            remote(buf.at[partner], buf.at[partner], ssem.at[3 + d], rsem.at[3 + d], along_y(d)).start()

    def share_finish(buf, ssem, rsem):
        for d in range(1, 4):
            for half in range(2):
                remote(
                    buf.at[blk], buf.at[(hi if half == 0 else 1 - hi) * 4 + y_at[4 - d]], ssem.at[d - 1 + 4 * half],
                    rsem.at[d - 1 + 4 * half], across,
                ).wait_recv()

    def share_sent(buf, ssem, rsem):
        for s in range(7):
            remote(buf.at[blk], buf.at[blk], ssem.at[s], rsem.at[s], across).wait_send()

    share_start(toks, tok_out, tok_in)

    for dz in (4, -3, 3, -2, 2, -1, 1):
        remote(slices.at[z_blk[dz]], wall.at[exp], qa_out.at[0], qa_in.at[dz + 3], along_z(dz)).start()

    def pass_on(slot, buf, ssem, rsem):
        row = source_row(slot)
        for d in range(1, 4):
            remote(buf.at[row], buf.at[row], ssem.at[0], rsem.at[0], along_x(d)).start()

    pass_on(3, wall, qb_out, qb_in)

    loads[11].wait()
    for dz in (4, -3, 3, -2, 2, -1, 1):
        remote(wout.at[exp], wout.at[exp], oa_out.at[0], oa_in.at[dz + 3], along_z(dz)).start()
    for dz in (1, -1, 2, -2, 3, -3, 4):
        row = source_row(dz + 3)
        remote(wall.at[row], wall.at[row], qa_out.at[0], qa_in.at[dz + 3], across).wait_recv()
        pass_on(dz + 3, wall, qb_out, qb_in)
    share_forward(toks, tok_out, tok_in)
    for n in range(4, 9):
        loads[n].wait()
    lane = lax.broadcasted_iota(jnp.int32, (ROWS, 128), 1)
    line = lax.broadcasted_iota(jnp.int32, (ROWS, 128), 0)
    parent = jnp.concatenate([par_ref[0:1, :], par_ref[1:2, :]], axis=1)
    parent = jnp.where(parent >= 0, parent + 64 * (lax.broadcasted_iota(jnp.int32, (1, 128), 1) // 64), -1)
    eye = jnp.where(lane == line, 1.0, 0.0)
    upward = eye + jnp.where(line == parent, 1.0, 0.0)
    for doubling in range(6):
        short = upward.astype(bf)
        upward = jnp.minimum(upward + jnp.dot(short, short, preferred_element_type=f32), 1.0)
    upward_bf = upward.astype(bf)
    dims0 = (((0,), (0,)), ((), ()))
    reach = lax.dot_general(upward_bf, eye.astype(bf), dims0, preferred_element_type=f32)
    depth = lax.dot_general(upward_bf, jnp.ones((ROWS, 128), bf), dims0, preferred_element_type=f32) - 1.0
    len0 = len_ref[0].astype(f32)
    len1 = len_ref[1].astype(f32)
    place = depth + jnp.where(line < 64, len0, len1)
    rate = jnp.exp((lane % 32).astype(f32) * (-9.210340371976184 / 32.0))
    angle = place * rate
    cos = jnp.cos(angle)
    low_half = (lane % 64) < 32
    sin = jnp.where(low_half, -1.0, 1.0) * jnp.sin(angle)
    target = jnp.sum(upward, axis=0, keepdims=True) - 1.0 + jnp.where(lane[0:1] < 64, len0, len1)
    on_path = jnp.sum(
        jnp.where((line == leaf_ref[0]) | (line == leaf_ref[1] + 64), reach, 0.0), axis=0, keepdims=True
    )

    share_finish(toks, tok_out, tok_in)

    for r in range(2):
        rows = toks[:, r].reshape(TREE, D_MODEL).astype(f32)
        scale = lax.rsqrt(jnp.mean(rows * rows, axis=-1, keepdims=True) + 1e-06)
        normed_ref[r * TREE : (r + 1) * TREE, :] = (rows * scale).astype(bf)
    remote(wall.at[pl.ds(0, 24)], wall.at[pl.ds(0, 24)], qb_out.at[0], qb_in.at[0], across).wait_recv()
    w_first = wall[:, :, 0:128].reshape(D_MODEL, 128)
    w_second = wall[:, :, 128:256].reshape(D_MODEL, 128)
    first = jnp.dot(normed_ref[...], w_first, preferred_element_type=f32)
    turned = jnp.where(low_half, pltpu.roll(first, 96, 1), pltpu.roll(first, 32, 1))
    made[blk, 0:ROWS, :] = (first * cos + turned * sin).astype(bf)
    quarter = normed_ref[pl.ds(pl.multiple_of(y * 32, 32), 32), :]
    made[blk, ROWS:CARRIED, :] = jnp.dot(quarter, w_second, preferred_element_type=f32).astype(bf)

    share_start(made, made_out, made_in)

    pass_on(3, wout, ob_out, ob_in)
    rows = 16
    mine = pl.ds(pl.multiple_of(tp * HALF, HALF), HALF)
    theirs = pl.ds(pl.multiple_of((1 - tp) * HALF, HALF), HALF)
    slot = lax.broadcasted_iota(jnp.int32, (SLOTS * SLAB, rows), 0)
    kk = slot // SLAB
    cc = slot % SLAB
    expert_of = ((z_lo + kk // 4 + 5) % 8) * 4 + (x + kk % 4) % 4
    named = jnp.zeros((SLOTS * SLAB, rows), f32)
    weighed = jnp.zeros((SLOTS * SLAB, rows), f32)
    for t in range(8):
        hit = expert_of == routes_ref[t : t + 1, :]
        named = named + jnp.where(hit, 1.0, 0.0)
        weighed = weighed + jnp.where(hit, weight_ref[t : t + 1, :], 0.0)
    earlier = jnp.where(
        lax.broadcasted_iota(jnp.int32, (rows, rows), 0) < lax.broadcasted_iota(jnp.int32, (rows, rows), 1), 1.0, 0.0
    ).astype(bf)
    rank = jnp.dot(named.astype(bf), earlier, preferred_element_type=f32)
    chosen = jnp.where((named > 0.5) & (jnp.abs(rank - cc.astype(f32)) < 0.5), 1.0, 0.0)
    weighed = weighed * chosen
    chosen_bf = chosen.astype(bf)
    w_high = weighed.astype(bf)
    w_low = (weighed - w_high.astype(f32)).astype(bf)

    share_forward(made, made_out, made_in)
    for dz in (1, -1, 2, -2, 3, -3, 4):
        row = source_row(dz + 3)
        remote(wout.at[row], wout.at[row], oa_out.at[0], oa_in.at[dz + 3], across).wait_recv()
        pass_on(dz + 3, wout, ob_out, ob_in)
    share_finish(made, made_out, made_in)

    for n in (9, 10):
        loads[n].wait()
    tree_k = [made[6 + c, 0:ROWS, :] for c in range(2)]
    tree_v = [jnp.concatenate([made[c * 4 + q, ROWS:CARRIED, :] for q in range(4)], axis=0) for c in range(2)]
    nt = (((1,), (1,)), ((), ()))
    left = lane < 64
    for r in range(2):
        length = len0 if r == 0 else len1
        sees = (lane[0:1] + blk * 128).astype(f32) < length
        tree_ok = (reach[r * TREE : (r + 1) * TREE] > 0.5) & (((lane[0:TREE] % 64) // 8) == blk)
        left64 = left[0:TREE]
        lane64 = lane[0:TREE]
        stat = jnp.zeros((TREE, 128), f32)
        tops = []
        for c in range(2):
            stack = []
            for head in range(6 * c, 6 * c + 6):
                block = made[head // 2, r * TREE : (r + 1) * TREE, :].astype(f32)
                side = (head // 3) % 2
                if side != head % 2:
                    block = pltpu.roll(block, 64, 1)
                stack.append(jnp.where(left64 if side == 0 else ~left64, block, 0.0).astype(bf))
            query = jnp.concatenate(stack, axis=0)
            cols = slice(c * 128, (c + 1) * 128)
            s_cache = lax.dot_general(query, ck_ref[r, :, cols], nt, preferred_element_type=f32) * score_scale
            s_tree = lax.dot_general(query, tree_k[c], nt, preferred_element_type=f32) * score_scale
            s_cache = jnp.where(sees, s_cache, masked_score).reshape(6, TREE, 128)
            s_tree = jnp.where(tree_ok, s_tree.reshape(6, TREE, 128), masked_score)
            peak = jnp.maximum(
                jnp.max(s_cache, axis=-1, keepdims=True), jnp.max(s_tree, axis=-1, keepdims=True)
            )
            p_cache = jnp.where(sees, jnp.exp(s_cache - peak), 0.0)
            p_tree = jnp.where(tree_ok, jnp.exp(s_tree - peak), 0.0)
            mass = jnp.sum(p_cache, axis=-1, keepdims=True) + jnp.sum(p_tree, axis=-1, keepdims=True)
            total = jnp.dot(
                p_cache.reshape(6 * TREE, 128).astype(bf), cv_ref[r, :, cols], preferred_element_type=f32
            ) + jnp.dot(p_tree.reshape(6 * TREE, 128).astype(bf), tree_v[c], preferred_element_type=f32)
            total = total.reshape(6, TREE, 128) / jnp.where(mass > 0.0, mass, 1.0)
            for n in range(6):
                head = 6 * c + n
                stat = jnp.where(lane64 == head, peak[n], stat)
                stat = jnp.where(lane64 == 64 + head, mass[n], stat)
                tops.append(total[n])
        for i in range(6):
            parts = []
            for u in range(2):
                head = 2 * i + u
                value = tops[head]
                if (head // 3) % 2 != u:
                    value = pltpu.roll(value, 64, 1)
                parts.append(value)
            joined = jnp.where(left64, parts[0], parts[1])
            part_send[:, :, r, :, i * 128 : (i + 1) * 128] = joined.astype(bf).reshape(2, 4, 8, 128)
        stat_send[:, :, r, :, :] = stat.reshape(2, 4, 8, 128)

    for group, other in ((0, 1 - hi), (1, hi)):
        for d in range(1, 4):
            remote(
                part_send.at[other, y_at[d]], near_recv.at[group, y], part_sem.at[4 * group], part_sem.at[4 * group + 1],
                along_y(d),
            ).start()
            remote(
                stat_send.at[other, y_at[d]], near_stat.at[group, y], part_sem.at[4 * group + 2],
                part_sem.at[4 * group + 3], along_y(d),
            ).start()
        near_recv[group, y] = part_send[other, y]
        near_stat[group, y] = stat_send[other, y]

    spread = jnp.where(
        lax.broadcasted_iota(jnp.int32, (128, HALF), 1) // 64 == lax.broadcasted_iota(jnp.int32, (128, HALF), 0), 1.0, 0.0
    ).astype(bf)

    def combine(count, stats, values):
        masses = pltpu.roll(stats.reshape(count * 16, 128), 64, 1).reshape(count, 16, 128)
        peak = jnp.max(stats, axis=0, keepdims=True)
        share = jnp.where(lane[0:16] < 12, masses * jnp.exp(stats - peak), 0.0)
        whole = jnp.sum(share, axis=0, keepdims=True)
        share = (share / jnp.where(whole > 0.0, whole, 1.0)).reshape(count * 16, 128)
        share_high = share.astype(bf)
        share_low = (share - share_high.astype(f32)).astype(bf)
        factor = jnp.dot(share_high, spread, preferred_element_type=f32) + jnp.dot(
            share_low, spread, preferred_element_type=f32
        )
        joined = jnp.sum(factor.reshape(count, 16, HALF) * values.reshape(count, 16, HALF).astype(f32), axis=0)
        stat = jnp.where(lane[0:16] < 12, peak[0], 0.0) + pltpu.roll(whole[0], 64, 1)
        return joined, stat

    def near_wait(group):
        for n, (out, into) in enumerate(((part_send.at[0], near_recv.at[group]), (stat_send.at[0], near_stat.at[group]))):
            remote(
                out.at[pl.ds(0, 3)], into.at[pl.ds(0, 3)], part_sem.at[4 * group + 2 * n],
                part_sem.at[4 * group + 2 * n + 1], across,
            ).wait()

    near_wait(0)
    joined, stat = combine(4, near_stat[0].reshape(4, 16, 128), near_recv[0])
    far_send[...] = joined.astype(bf)
    far_stat_send[...] = stat
    far = (
        remote(far_send, far_recv, part_sem.at[8], part_sem.at[9], across),
        remote(far_stat_send, far_stat, part_sem.at[10], part_sem.at[11], across),
    )
    for copy in far:
        copy.start()
    for r in range(2):
        spot = (line + blk * 128).astype(f32)
        placing = jnp.where((spot == target) & (on_path > 0.5) & ((lane // 64) == r), 1.0, 0.0)
        written = jnp.max(placing, axis=-1, keepdims=True) > 0.5
        placing = placing.astype(bf)
        for c in range(2):
            cols = slice(c * 128, (c + 1) * 128)
            moved_k = jnp.dot(placing, tree_k[c], preferred_element_type=f32)
            nk_ref[r, :, cols] = jnp.where(written, moved_k, ck_ref[r, :, cols].astype(f32)).astype(bf)
            moved_v = jnp.dot(placing, tree_v[c], preferred_element_type=f32)
            nv_ref[r, :, cols] = jnp.where(written, moved_v, cv_ref[r, :, cols].astype(f32)).astype(bf)
    near_wait(1)
    joined, stat = combine(4, near_stat[1].reshape(4, 16, 128), near_recv[1])
    for copy in far:
        copy.wait()
    first_peak = stat
    second_peak = far_stat[...]
    peak = jnp.maximum(first_peak, second_peak)
    pair_share = [
        jnp.where(lane[0:16] < 12, pltpu.roll(one, 64, 1) * jnp.exp(one - peak), 0.0) for one in (first_peak, second_peak)
    ]
    whole = pair_share[0] + pair_share[1]
    inverse = 1.0 / jnp.where(whole > 0.0, whole, 1.0)
    pair_share = jnp.concatenate([pair_share[0] * inverse, pair_share[1] * inverse], axis=0)
    share_high = pair_share.astype(bf)
    share_low = (pair_share - share_high.astype(f32)).astype(bf)
    factor = jnp.dot(share_high, spread, preferred_element_type=f32) + jnp.dot(
        share_low, spread, preferred_element_type=f32
    )
    context = (factor[0:16] * joined + factor[16:32] * far_recv[...].astype(f32)).astype(bf)
    remote(wout.at[pl.ds(0, 24)], wout.at[pl.ds(0, 24)], ob_out.at[0], ob_in.at[0], across).wait_recv()
    terms = lax.dot_general(context, wout[...].reshape(D_MODEL, HALF), nt, preferred_element_type=f32).astype(bf)
    pair_send[...] = terms
    pair = remote(pair_send, pair_recv, pair_sem.at[0], pair_sem.at[1], sibling)
    pair.start()
    pair.wait()
    attended = (terms.astype(f32) + pair_recv[...].astype(f32)).astype(bf)
    att_ref[...] = attended
    mixed = tok_ref[...].reshape(16, D_MODEL).astype(f32) + residual_scale * attended.astype(f32)
    scale = lax.rsqrt(jnp.mean(mixed * mixed, axis=-1, keepdims=True) + 1e-06)
    hidden_in = (mixed * scale).astype(bf)
    for own in range(2):

        @pl.when(tp == own)
        def _():
            sent = jnp.dot(chosen_bf, hidden_in[:, own * HALF : (own + 1) * HALF], preferred_element_type=f32).astype(bf)
            send[...] = sent.reshape(SLOTS, SLAB, HALF)

    recv[tp, OWN_SLOT] = send[OWN_SLOT]
    order = sorted(range(-3, 5), key=lambda d: -abs(d))
    for dz in order:
        for dx in (2, 1, 3, 0):
            k = (dz + 3) * 4 + dx
            if k != OWN_SLOT:
                remote(send.at[k], recv.at[tp, k], ship_out.at[0], ship_in.at[0], plane(dz, dx)).start()
    remote(
        send.at[pl.ds(0, 31)], recv.at[tp, pl.ds(0, 31)], ship_out.at[0], ship_in.at[0], sibling
    ).wait()
    swap = remote(recv.at[tp], recv.at[tp], pair_sem.at[2], pair_sem.at[3], sibling)
    swap.start()
    for n in (12, 13):
        loads[n].wait()
    swap.wait()
    low = recv[0].reshape(SLOTS * SLAB, HALF)
    high = recv[1].reshape(SLOTS * SLAB, HALF)

    def proj(g):
        return jnp.dot(low, wgu[g, :HALF, :], preferred_element_type=f32) + jnp.dot(
            high, wgu[g, HALF:, :], preferred_element_type=f32
        )

    gate = proj(0)
    up = proj(1)
    hidden = (gate / (1.0 + jnp.exp(-gate)) * up).astype(bf)
    half_send[...] = jnp.dot(hidden, wdn[:, theirs], preferred_element_type=f32).astype(bf)
    swap = remote(half_send, half_recv, pair_sem.at[4], pair_sem.at[5], sibling)
    swap.start()
    part = jnp.dot(hidden, wdn[:, mine], preferred_element_type=f32)
    swap.wait()
    total = (part + half_recv[...].astype(f32)).astype(bf)
    back_send[...] = total.reshape(SLOTS, SLAB, HALF)
    back_recv[OWN_SLOT] = total[OWN_SLOT * SLAB : (OWN_SLOT + 1) * SLAB]
    for dz in order:
        for dx in (2, 1, 3, 0):
            k = (dz + 3) * 4 + dx
            if k != OWN_SLOT:
                remote(
                    back_send.at[k], back_recv.at[k], ship_out.at[1], ship_in.at[1], plane(-dz, (4 - dx) % 4)
                ).start()
    remote(
        back_send.at[pl.ds(0, 31)], back_recv.at[pl.ds(0, 31)], ship_out.at[1], ship_in.at[1], sibling
    ).wait()
    got = back_recv[...].reshape(SLOTS * SLAB, HALF)
    combined = lax.dot_general(w_high, got, dims0, preferred_element_type=f32) + lax.dot_general(
        w_low, got, dims0, preferred_element_type=f32
    )
    fin_send[...] = combined.astype(bf)
    last = remote(fin_send, fin_recv, pair_sem.at[6], pair_sem.at[7], sibling)
    last.start()
    mix_ref[:, mine] = combined.astype(bf)
    last.wait()
    mix_ref[:, theirs] = fin_recv[...]

    share_sent(toks, tok_out, tok_in)
    share_sent(made, made_out, made_in)
    remote(wall.at[pl.ds(0, 7)], wall.at[pl.ds(0, 7)], qa_out.at[0], qb_in.at[0], across).wait_send()
    remote(wall.at[pl.ds(0, 24)], wall.at[pl.ds(0, 24)], qb_out.at[0], qb_in.at[0], across).wait_send()
    remote(wout.at[pl.ds(0, 7)], wout.at[pl.ds(0, 7)], oa_out.at[0], ob_in.at[0], across).wait_send()
    remote(wout.at[pl.ds(0, 24)], wout.at[pl.ds(0, 24)], ob_out.at[0], ob_in.at[0], across).wait_send()


def local(tokens, w_query, w_key, w_value, w_out, cache_keys, cache_values, parents, lengths, accepted_leaf, routes,
          route_weight, w_gateup, w_down):
    f32, bf = jnp.float32, jnp.bfloat16
    vmem = pltpu.VMEM
    keep = pl.BlockSpec(memory_space=pltpu.VMEM)
    dma = pltpu.SemaphoreType.DMA
    attended, expert_mix, new_keys, new_values = pl.pallas_call(
        layer_kernel,
        out_shape=(
            jax.ShapeDtypeStruct(tokens.shape, bf),
            jax.ShapeDtypeStruct(tokens.shape, bf),
            jax.ShapeDtypeStruct(cache_keys.shape, bf),
            jax.ShapeDtypeStruct(cache_values.shape, bf),
        ),
        in_specs=[pl.BlockSpec(memory_space=pl.ANY)] * 14,
        out_specs=(keep,) * 4,
        scratch_shapes=[
            pltpu.SMEM((2,), jnp.int32), pltpu.SMEM((2,), jnp.int32),
            vmem((2, 8, D_MODEL), bf), vmem((48, HALF), bf), vmem((48, 256), bf), vmem((48, 256), bf),
            vmem((2, 128, 256), bf), vmem((2, 128, 256), bf), vmem((2, TREE), jnp.int32), vmem((8, 16), jnp.int32),
            vmem((8, 16), f32), vmem((2, D_MODEL, 256), bf), vmem((256, D_MODEL), bf),
            vmem((8, 2, 8, D_MODEL), bf), vmem((8, 48, 256), bf), vmem((32, 48, 256), bf), vmem((32, 48, HALF), bf),
            vmem((ROWS, D_MODEL), bf), vmem((8, CARRIED, 128), bf),
            vmem((2, 4, 2, 8, HALF), bf), vmem((2, 4, 2, 8, HALF), bf), vmem((2, 4, 2, 8, 128), f32),
            vmem((2, 4, 2, 8, 128), f32), vmem((16, HALF), bf), vmem((16, HALF), bf), vmem((16, 128), f32),
            vmem((16, 128), f32), vmem((16, D_MODEL), bf), vmem((16, D_MODEL), bf),
            vmem((SLOTS, SLAB, HALF), bf), vmem((2, SLOTS, SLAB, HALF), bf), vmem((SLOTS * SLAB, HALF), bf),
            vmem((SLOTS * SLAB, HALF), bf), vmem((SLOTS, SLAB, HALF), bf), vmem((SLOTS, SLAB, HALF), bf),
            vmem((16, HALF), bf), vmem((16, HALF), bf),
            dma((14,)), dma((7,)), dma((7,)), dma((7,)), dma((7,)),
            dma((1,)), dma((8,)), dma((1,)), dma((1,)),
            dma((1,)), dma((8,)), dma((1,)), dma((1,)),
            dma((12,)), dma((8,)), dma((2,)), dma((2,)),
        ],
        compiler_params=pltpu.CompilerParams(
            collective_id=1, has_side_effects=True, vmem_limit_bytes=50 * 1024 * 1024
        ),
    )(
        lengths, accepted_leaf, tokens.reshape(2, 8, D_MODEL), w_query, w_key, w_value, cache_keys, cache_values, parents,
        w_out.T, routes.T, route_weight.T, w_gateup[0].transpose(1, 0, 2), w_down[0],
    )
    return (attended, expert_mix, new_keys, new_values)


def solution(mesh):
    in_specs = (
        P(("blk", "expert"), None),
        P("expert", "tp"),
        P("expert", "tp"),
        P("expert", "tp"),
        P("tp", "expert"),
        P("expert", "blk", "tp"),
        P("expert", "blk", "tp"),
        P("expert", None),
        P("expert"),
        P("expert"),
        P(("blk", "expert"), None),
        P(("blk", "expert"), None),
        P("expert", None, None, "tp"),
        P("expert", "tp", None),
    )
    out_specs = (
        P(("blk", "expert"), None),
        P(("blk", "expert"), None),
        P("expert", "blk", "tp"),
        P("expert", "blk", "tp"),
    )
    return jax.shard_map(local, mesh=mesh, in_specs=in_specs, out_specs=out_specs, check_vma=False)
```

```python
import jax
import jax.numpy as jnp
from jax import lax
from jax.experimental import pallas as pl
from jax.experimental.pallas import tpu as pltpu
from jax.sharding import PartitionSpec as P

score_scale = 0.015625
residual_scale = 0.22
masked_score = -1e30
D_MODEL = 1536
HALF = 768
SLOTS = 32
OWN_SLOT = 12
SLAB = 8
TREE = 64
ROWS = 128
CARRIED = 160
PACKED = 64
MESH = pl.DeviceIdType.MESH


def layer_kernel(len_hbm, leaf_hbm, tok_hbm, wq_hbm, wk_hbm, wv_hbm, ck_hbm, cv_hbm, par_hbm, wo_hbm, routes_hbm, weight_hbm,
                 wgu_hbm, wdn_hbm, att_ref, mix_ref, nk_ref, nv_ref, len_ref, leaf_ref, tok_ref, wq_ref, wk_ref, wv_ref,
                 ck_ref, cv_ref, par_ref, routes_ref, weight_ref, wgu, wdn, toks, slices, wall, wout, normed_ref, made,
                 part_send, near_recv, stat_send, near_stat, far_send, far_recv, far_stat_send, far_stat, pair_send,
                 pair_recv, send, recv, half_send, half_recv, back_send, back_recv, fin_send, fin_recv, load_sem, tok_out,
                 tok_in, made_out, made_in, qa_out, qa_in, qb_out, qb_in, oa_out, oa_in, ob_out, ob_in, oy_out, oy_in, part_sem,
                 pair_sem, ship_out, ship_in):
    f32, bf = jnp.float32, jnp.bfloat16
    blk = lax.axis_index("blk")
    exp = lax.axis_index("expert")
    tp = lax.axis_index("tp")
    hi = lax.div(blk, 4)
    y = lax.rem(blk, 4)
    z_lo = lax.div(exp, 4)
    z = hi * 8 + z_lo
    x = lax.rem(exp, 4)
    partner = (1 - hi) * 4 + y
    z_blk, z_exp = {}, {}
    for dz in range(-4, 5):
        zz = lax.rem(z + (dz + 16), 16)
        z_blk[dz] = lax.div(zz, 8) * 4 + y
        z_exp[dz] = lax.rem(zz, 8) * 4
    x_at = {dx: lax.rem(x + dx, 4) for dx in range(4)}
    y_at = {dy: lax.rem(y + dy, 4) for dy in range(4)}

    def plane(dz, dx):
        return (z_blk[dz], z_exp[dz] + x_at[dx], tp)

    def along_z(dz):
        return plane(dz, 0)

    def along_x(dx):
        return plane(0, dx)

    def along_y(dy):
        return (hi * 4 + y_at[dy], exp, tp)

    across = (partner, exp, tp)
    sibling = (blk, exp, 1 - tp)

    def source_row(slot):
        return lax.rem(z_lo + (11 - slot), 8) * 4 + x

    def remote(src, dst, ssem, rsem, device):
        return pltpu.make_async_remote_copy(
            src_ref=src, dst_ref=dst, send_sem=ssem, recv_sem=rsem, device_id=device, device_id_type=MESH
        )

    pairs = (
        (wq_hbm, wq_ref), (wk_hbm, wk_ref), (wv_hbm, wv_ref), (tok_hbm, tok_ref), (len_hbm, len_ref),
        (leaf_hbm, leaf_ref), (par_hbm, par_ref), (routes_hbm, routes_ref), (weight_hbm, weight_ref), (ck_hbm, ck_ref),
        (cv_hbm, cv_ref), (wo_hbm, wout.at[exp]), (wgu_hbm, wgu), (wdn_hbm, wdn),
    )
    loads = [pltpu.make_async_copy(src, dst, load_sem.at[n]) for n, (src, dst) in enumerate(pairs)]
    parity = lax.rem(y, 2)
    gives = lax.rem(z_lo + y, 2) == 0
    for n, load in enumerate(loads):
        if n == 11:
            pl.when(gives)(load.start)
        else:
            load.start()

    barrier = pltpu.get_barrier_semaphore()

    def greet(device):
        pl.semaphore_signal(barrier, inc=1, device_id=device, device_id_type=MESH)

    for d in range(1, 8):
        greet((lax.rem(blk + d, 8), exp, tp))
    for dz in (-4, 4, -3, 3, -2, 2, -1, 1, 0):
        for dx in range(4):
            if dz or dx:
                greet(plane(dz, dx))
    greet(sibling)

    for n in range(4):
        loads[n].wait()
    group16 = lax.broadcasted_iota(jnp.int32, (16, 128), 1) // 32
    for b in range(8):
        if b < 6:
            slices[b, 0:48, :] = wq_ref[:, b * 128 : (b + 1) * 128]
        else:
            slices[b, 0:48, :] = wk_ref[:, (b - 6) * 128 : (b - 5) * 128]
        fold = jnp.zeros((16, 128), f32)
        for g in range(3):
            piece = wv_ref[16 * g : 16 * g + 16, (b // 4) * 128 : (b // 4 + 1) * 128].astype(f32)
            turn = (32 * (g - b % 4)) % 128
            piece = pltpu.roll(piece, turn, 1) if turn else piece
            fold = jnp.where(group16 == g, piece, fold)
        slices[b, 48:PACKED, :] = fold.astype(bf)
    wall[exp] = slices[blk]
    toks[blk] = tok_ref[...]
    pl.semaphore_wait(barrier, 43)

    def share_start(buf, ssem, rsem):
        remote(buf.at[blk], buf.at[blk], ssem.at[3], rsem.at[3], across).start()
        for d in range(1, 4):
            remote(buf.at[blk], buf.at[blk], ssem.at[d - 1], rsem.at[d - 1], along_y(d)).start()

    def share_forward(buf, ssem, rsem):
        remote(buf.at[partner], buf.at[partner], ssem.at[3], rsem.at[3], across).wait_recv()
        for d in range(1, 4):
            remote(buf.at[partner], buf.at[partner], ssem.at[3 + d], rsem.at[3 + d], along_y(d)).start()

    def share_finish(buf, ssem, rsem):
        for d in range(1, 4):
            for half in range(2):
                remote(
                    buf.at[blk], buf.at[(hi if half == 0 else 1 - hi) * 4 + y_at[4 - d]], ssem.at[d - 1 + 4 * half],
                    rsem.at[d - 1 + 4 * half], across,
                ).wait_recv()

    def share_sent(buf, ssem, rsem):
        for s in range(7):
            remote(buf.at[blk], buf.at[blk], ssem.at[s], rsem.at[s], across).wait_send()

    share_start(toks, tok_out, tok_in)

    for dz in (4, -3, 3, -2, 2, -1, 1):
        remote(slices.at[z_blk[dz]], wall.at[exp], qa_out.at[0], qa_in.at[dz + 3], along_z(dz)).start()

    def pass_on(slot, buf, ssem, rsem):
        row = source_row(slot)
        for d in range(1, 4):
            remote(buf.at[row], buf.at[row], ssem.at[0], rsem.at[0], along_x(d)).start()

    pass_on(3, wall, qb_out, qb_in)

    @pl.when(gives)
    def _():
        loads[11].wait()
        for dz in (4, -3, 3, -2, 2, -1, 1):
            remote(wout.at[exp], wout.at[exp], oa_out.at[0], oa_in.at[dz + 3], along_z(dz)).start()

    for dz in (1, -1, 2, -2, 3, -3, 4):
        row = source_row(dz + 3)
        remote(wall.at[row], wall.at[row], qa_out.at[0], qa_in.at[dz + 3], across).wait_recv()
        pass_on(dz + 3, wall, qb_out, qb_in)
    share_forward(toks, tok_out, tok_in)
    for n in range(4, 9):
        loads[n].wait()
    lane = lax.broadcasted_iota(jnp.int32, (ROWS, 128), 1)
    line = lax.broadcasted_iota(jnp.int32, (ROWS, 128), 0)
    parent = jnp.concatenate([par_ref[0:1, :], par_ref[1:2, :]], axis=1)
    parent = jnp.where(parent >= 0, parent + 64 * (lax.broadcasted_iota(jnp.int32, (1, 128), 1) // 64), -1)
    eye = jnp.where(lane == line, 1.0, 0.0)
    upward = eye + jnp.where(line == parent, 1.0, 0.0)
    for doubling in range(6):
        short = upward.astype(bf)
        upward = jnp.minimum(upward + jnp.dot(short, short, preferred_element_type=f32), 1.0)
    upward_bf = upward.astype(bf)
    dims0 = (((0,), (0,)), ((), ()))
    reach = lax.dot_general(upward_bf, eye.astype(bf), dims0, preferred_element_type=f32)
    depth = lax.dot_general(upward_bf, jnp.ones((ROWS, 128), bf), dims0, preferred_element_type=f32) - 1.0
    len0 = len_ref[0].astype(f32)
    len1 = len_ref[1].astype(f32)
    place = depth + jnp.where(line < 64, len0, len1)
    rate = jnp.exp((lane % 32).astype(f32) * (-9.210340371976184 / 32.0))
    angle = place * rate
    cos = jnp.cos(angle)
    low_half = (lane % 64) < 32
    sin = jnp.where(low_half, -1.0, 1.0) * jnp.sin(angle)
    target = jnp.sum(upward, axis=0, keepdims=True) - 1.0 + jnp.where(lane[0:1] < 64, len0, len1)
    on_path = jnp.sum(
        jnp.where((line == leaf_ref[0]) | (line == leaf_ref[1] + 64), reach, 0.0), axis=0, keepdims=True
    )

    share_finish(toks, tok_out, tok_in)

    for r in range(2):
        rows = toks[:, r].reshape(TREE, D_MODEL).astype(f32)
        scale = lax.rsqrt(jnp.mean(rows * rows, axis=-1, keepdims=True) + 1e-06)
        normed_ref[r * TREE : (r + 1) * TREE, :] = (rows * scale).astype(bf)
    remote(wall.at[pl.ds(0, 24)], wall.at[pl.ds(0, 24)], qb_out.at[0], qb_in.at[0], across).wait_recv()
    w_first = wall[:, 0:48, :].reshape(D_MODEL, 128)
    folded = wall[:, 48:PACKED, :].astype(f32)
    group = lax.broadcasted_iota(jnp.int32, (32, 16, 128), 2) // 32
    w_second = jnp.concatenate([jnp.where(group == g, folded, 0.0) for g in range(3)], axis=1)
    w_second = w_second.astype(bf).reshape(D_MODEL, 128)
    first = jnp.dot(normed_ref[...], w_first, preferred_element_type=f32)
    turned = jnp.where(low_half, pltpu.roll(first, 96, 1), pltpu.roll(first, 32, 1))
    made[blk, 0:ROWS, :] = (first * cos + turned * sin).astype(bf)
    second = jnp.dot(normed_ref[...], w_second, preferred_element_type=f32)
    second = second + pltpu.roll(second, 96, 1) + pltpu.roll(second, 64, 1)
    line_group = lane[0:32] // 32
    carried = jnp.zeros((32, 128), f32)
    for q in range(4):
        piece = second[32 * q : 32 * q + 32]
        piece = pltpu.roll(piece, 32 * q, 1) if q else piece
        carried = jnp.where(line_group == q, piece, carried)
    made[blk, ROWS:CARRIED, :] = carried.astype(bf)

    share_start(made, made_out, made_in)

    for dz in (0, 1, -1, 2, -2, 3, -3, 4):
        row = source_row(dz + 3)
        source_z = lax.rem(z_lo + (8 - dz), 8)

        @pl.when(lax.rem(source_z + parity, 2) == 0)
        def _(dz=dz, row=row, source_z=source_z):
            if dz:
                remote(wout.at[row], wout.at[row], oa_out.at[0], oa_in.at[dz + 3], across).wait_recv()
            for d in range(1, 4):
                remote(
                    wout.at[row], wout.at[row], ob_out.at[0], ob_in.at[lax.div(source_z, 2)], along_x(d)
                ).start()
            near_y = (hi * 4 + lax.rem(y + 1 + 2 * lax.div(source_z, 4), 4), exp, tp)
            remote(wout.at[row], wout.at[row], oy_out.at[0], oy_in.at[0], near_y).start()

    rows = 16
    mine = pl.ds(pl.multiple_of(tp * HALF, HALF), HALF)
    theirs = pl.ds(pl.multiple_of((1 - tp) * HALF, HALF), HALF)
    slot = lax.broadcasted_iota(jnp.int32, (SLOTS * SLAB, rows), 0)
    kk = slot // SLAB
    cc = slot % SLAB
    expert_of = ((z_lo + kk // 4 + 5) % 8) * 4 + (x + kk % 4) % 4
    named = jnp.zeros((SLOTS * SLAB, rows), f32)
    weighed = jnp.zeros((SLOTS * SLAB, rows), f32)
    for t in range(8):
        hit = expert_of == routes_ref[t : t + 1, :]
        named = named + jnp.where(hit, 1.0, 0.0)
        weighed = weighed + jnp.where(hit, weight_ref[t : t + 1, :], 0.0)
    earlier = jnp.where(
        lax.broadcasted_iota(jnp.int32, (rows, rows), 0) < lax.broadcasted_iota(jnp.int32, (rows, rows), 1), 1.0, 0.0
    ).astype(bf)
    rank = jnp.dot(named.astype(bf), earlier, preferred_element_type=f32)
    chosen = jnp.where((named > 0.5) & (jnp.abs(rank - cc.astype(f32)) < 0.5), 1.0, 0.0)
    weighed = weighed * chosen
    chosen_bf = chosen.astype(bf)
    w_high = weighed.astype(bf)
    w_low = (weighed - w_high.astype(f32)).astype(bf)

    share_forward(made, made_out, made_in)
    share_finish(made, made_out, made_in)

    for n in (9, 10):
        loads[n].wait()
    tree_k = [made[6 + c, 0:ROWS, :] for c in range(2)]
    tree_v = []
    for c in range(2):
        quarters = []
        for q in range(4):
            whole = jnp.zeros((32, 128), f32)
            for g in range(4):
                piece = made[4 * c + g, ROWS:CARRIED, :].astype(f32)
                turn = (32 * (g - q)) % 128
                piece = pltpu.roll(piece, turn, 1) if turn else piece
                whole = jnp.where(line_group == g, piece, whole)
            quarters.append(whole)
        tree_v.append(jnp.concatenate(quarters, axis=0).astype(bf))
    nt = (((1,), (1,)), ((), ()))
    left = lane < 64
    for r in range(2):
        length = len0 if r == 0 else len1
        sees = (lane[0:1] + blk * 128).astype(f32) < length
        tree_ok = (reach[r * TREE : (r + 1) * TREE] > 0.5) & (((lane[0:TREE] % 64) // 8) == blk)
        left64 = left[0:TREE]
        lane64 = lane[0:TREE]
        stat = jnp.zeros((TREE, 128), f32)
        tops = []
        for c in range(2):
            stack = []
            for head in range(6 * c, 6 * c + 6):
                block = made[head // 2, r * TREE : (r + 1) * TREE, :].astype(f32)
                side = (head // 3) % 2
                if side != head % 2:
                    block = pltpu.roll(block, 64, 1)
                stack.append(jnp.where(left64 if side == 0 else ~left64, block, 0.0).astype(bf))
            query = jnp.concatenate(stack, axis=0)
            cols = slice(c * 128, (c + 1) * 128)
            s_cache = lax.dot_general(query, ck_ref[r, :, cols], nt, preferred_element_type=f32) * score_scale
            s_tree = lax.dot_general(query, tree_k[c], nt, preferred_element_type=f32) * score_scale
            s_cache = jnp.where(sees, s_cache, masked_score).reshape(6, TREE, 128)
            s_tree = jnp.where(tree_ok, s_tree.reshape(6, TREE, 128), masked_score)
            peak = jnp.maximum(
                jnp.max(s_cache, axis=-1, keepdims=True), jnp.max(s_tree, axis=-1, keepdims=True)
            )
            p_cache = jnp.where(sees, jnp.exp(s_cache - peak), 0.0)
            p_tree = jnp.where(tree_ok, jnp.exp(s_tree - peak), 0.0)
            mass = jnp.sum(p_cache, axis=-1, keepdims=True) + jnp.sum(p_tree, axis=-1, keepdims=True)
            total = jnp.dot(
                p_cache.reshape(6 * TREE, 128).astype(bf), cv_ref[r, :, cols], preferred_element_type=f32
            ) + jnp.dot(p_tree.reshape(6 * TREE, 128).astype(bf), tree_v[c], preferred_element_type=f32)
            total = total.reshape(6, TREE, 128) / jnp.where(mass > 0.0, mass, 1.0)
            for n in range(6):
                head = 6 * c + n
                stat = jnp.where(lane64 == head, peak[n], stat)
                stat = jnp.where(lane64 == 64 + head, mass[n], stat)
                tops.append(total[n])
        for i in range(6):
            parts = []
            for u in range(2):
                head = 2 * i + u
                value = tops[head]
                if (head // 3) % 2 != u:
                    value = pltpu.roll(value, 64, 1)
                parts.append(value)
            joined = jnp.where(left64, parts[0], parts[1])
            part_send[:, :, r, :, i * 128 : (i + 1) * 128] = joined.astype(bf).reshape(2, 4, 8, 128)
        stat_send[:, :, r, :, :] = stat.reshape(2, 4, 8, 128)

    for group, other in ((0, 1 - hi), (1, hi)):
        for d in range(1, 4):
            remote(
                part_send.at[other, y_at[d]], near_recv.at[group, y], part_sem.at[4 * group], part_sem.at[4 * group + 1],
                along_y(d),
            ).start()
            remote(
                stat_send.at[other, y_at[d]], near_stat.at[group, y], part_sem.at[4 * group + 2],
                part_sem.at[4 * group + 3], along_y(d),
            ).start()
        near_recv[group, y] = part_send[other, y]
        near_stat[group, y] = stat_send[other, y]

    spread = jnp.where(
        lax.broadcasted_iota(jnp.int32, (128, HALF), 1) // 64 == lax.broadcasted_iota(jnp.int32, (128, HALF), 0), 1.0, 0.0
    ).astype(bf)

    def combine(count, stats, values):
        masses = pltpu.roll(stats.reshape(count * 16, 128), 64, 1).reshape(count, 16, 128)
        peak = jnp.max(stats, axis=0, keepdims=True)
        share = jnp.where(lane[0:16] < 12, masses * jnp.exp(stats - peak), 0.0)
        whole = jnp.sum(share, axis=0, keepdims=True)
        share = (share / jnp.where(whole > 0.0, whole, 1.0)).reshape(count * 16, 128)
        share_high = share.astype(bf)
        share_low = (share - share_high.astype(f32)).astype(bf)
        factor = jnp.dot(share_high, spread, preferred_element_type=f32) + jnp.dot(
            share_low, spread, preferred_element_type=f32
        )
        joined = jnp.sum(factor.reshape(count, 16, HALF) * values.reshape(count, 16, HALF).astype(f32), axis=0)
        stat = jnp.where(lane[0:16] < 12, peak[0], 0.0) + pltpu.roll(whole[0], 64, 1)
        return joined, stat

    def near_wait(group):
        for n, (out, into) in enumerate(((part_send.at[0], near_recv.at[group]), (stat_send.at[0], near_stat.at[group]))):
            remote(
                out.at[pl.ds(0, 3)], into.at[pl.ds(0, 3)], part_sem.at[4 * group + 2 * n],
                part_sem.at[4 * group + 2 * n + 1], across,
            ).wait()

    for g in range(4):
        remote(wout.at[pl.ds(0, 3)], wout.at[pl.ds(0, 3)], ob_out.at[0], ob_in.at[g], across).wait_recv()
        for d in range(1, 4):
            row = (2 * g + parity) * 4 + x_at[d]
            remote(wout.at[row], wout.at[row], oy_out.at[0], oy_in.at[0], along_y(1 if g < 2 else 3)).start()
    near_wait(0)
    joined, stat = combine(4, near_stat[0].reshape(4, 16, 128), near_recv[0])
    far_send[...] = joined.astype(bf)
    far_stat_send[...] = stat
    far = (
        remote(far_send, far_recv, part_sem.at[8], part_sem.at[9], across),
        remote(far_stat_send, far_stat, part_sem.at[10], part_sem.at[11], across),
    )
    for copy in far:
        copy.start()
    for r in range(2):
        spot = (line + blk * 128).astype(f32)
        placing = jnp.where((spot == target) & (on_path > 0.5) & ((lane // 64) == r), 1.0, 0.0)
        written = jnp.max(placing, axis=-1, keepdims=True) > 0.5
        placing = placing.astype(bf)
        for c in range(2):
            cols = slice(c * 128, (c + 1) * 128)
            moved_k = jnp.dot(placing, tree_k[c], preferred_element_type=f32)
            nk_ref[r, :, cols] = jnp.where(written, moved_k, ck_ref[r, :, cols].astype(f32)).astype(bf)
            moved_v = jnp.dot(placing, tree_v[c], preferred_element_type=f32)
            nv_ref[r, :, cols] = jnp.where(written, moved_v, cv_ref[r, :, cols].astype(f32)).astype(bf)
    near_wait(1)
    joined, stat = combine(4, near_stat[1].reshape(4, 16, 128), near_recv[1])
    for copy in far:
        copy.wait()
    first_peak = stat
    second_peak = far_stat[...]
    peak = jnp.maximum(first_peak, second_peak)
    pair_share = [
        jnp.where(lane[0:16] < 12, pltpu.roll(one, 64, 1) * jnp.exp(one - peak), 0.0) for one in (first_peak, second_peak)
    ]
    whole = pair_share[0] + pair_share[1]
    inverse = 1.0 / jnp.where(whole > 0.0, whole, 1.0)
    pair_share = jnp.concatenate([pair_share[0] * inverse, pair_share[1] * inverse], axis=0)
    share_high = pair_share.astype(bf)
    share_low = (pair_share - share_high.astype(f32)).astype(bf)
    factor = jnp.dot(share_high, spread, preferred_element_type=f32) + jnp.dot(
        share_low, spread, preferred_element_type=f32
    )
    context = (factor[0:16] * joined + factor[16:32] * far_recv[...].astype(f32)).astype(bf)
    remote(wout.at[pl.ds(0, 16)], wout.at[pl.ds(0, 16)], oy_out.at[0], oy_in.at[0], across).wait()
    terms = lax.dot_general(context, wout[...].reshape(D_MODEL, HALF), nt, preferred_element_type=f32).astype(bf)
    pair_send[...] = terms
    pair = remote(pair_send, pair_recv, pair_sem.at[0], pair_sem.at[1], sibling)
    pair.start()
    pair.wait()
    attended = (terms.astype(f32) + pair_recv[...].astype(f32)).astype(bf)
    att_ref[...] = attended
    mixed = tok_ref[...].reshape(16, D_MODEL).astype(f32) + residual_scale * attended.astype(f32)
    scale = lax.rsqrt(jnp.mean(mixed * mixed, axis=-1, keepdims=True) + 1e-06)
    hidden_in = (mixed * scale).astype(bf)
    for own in range(2):

        @pl.when(tp == own)
        def _():
            sent = jnp.dot(chosen_bf, hidden_in[:, own * HALF : (own + 1) * HALF], preferred_element_type=f32).astype(bf)
            send[...] = sent.reshape(SLOTS, SLAB, HALF)

    recv[tp, OWN_SLOT] = send[OWN_SLOT]
    order = sorted(range(-3, 5), key=lambda d: -abs(d))
    for dz in order:
        for dx in (2, 1, 3, 0):
            k = (dz + 3) * 4 + dx
            if k != OWN_SLOT:
                remote(send.at[k], recv.at[tp, k], ship_out.at[0], ship_in.at[0], plane(dz, dx)).start()
    remote(
        send.at[pl.ds(0, 31)], recv.at[tp, pl.ds(0, 31)], ship_out.at[0], ship_in.at[0], sibling
    ).wait()
    swap = remote(recv.at[tp], recv.at[tp], pair_sem.at[2], pair_sem.at[3], sibling)
    swap.start()
    for n in (12, 13):
        loads[n].wait()
    swap.wait()
    low = recv[0].reshape(SLOTS * SLAB, HALF)
    high = recv[1].reshape(SLOTS * SLAB, HALF)

    def proj(g):
        return jnp.dot(low, wgu[g, :HALF, :], preferred_element_type=f32) + jnp.dot(
            high, wgu[g, HALF:, :], preferred_element_type=f32
        )

    gate = proj(0)
    up = proj(1)
    hidden = (gate / (1.0 + jnp.exp(-gate)) * up).astype(bf)
    half_send[...] = jnp.dot(hidden, wdn[:, theirs], preferred_element_type=f32).astype(bf)
    swap = remote(half_send, half_recv, pair_sem.at[4], pair_sem.at[5], sibling)
    swap.start()
    part = jnp.dot(hidden, wdn[:, mine], preferred_element_type=f32)
    swap.wait()
    total = (part + half_recv[...].astype(f32)).astype(bf)
    back_send[...] = total.reshape(SLOTS, SLAB, HALF)
    back_recv[OWN_SLOT] = total[OWN_SLOT * SLAB : (OWN_SLOT + 1) * SLAB]
    for dz in order:
        for dx in (2, 1, 3, 0):
            k = (dz + 3) * 4 + dx
            if k != OWN_SLOT:
                remote(
                    back_send.at[k], back_recv.at[k], ship_out.at[1], ship_in.at[1], plane(-dz, (4 - dx) % 4)
                ).start()
    remote(
        back_send.at[pl.ds(0, 31)], back_recv.at[pl.ds(0, 31)], ship_out.at[1], ship_in.at[1], sibling
    ).wait()
    got = back_recv[...].reshape(SLOTS * SLAB, HALF)
    combined = lax.dot_general(w_high, got, dims0, preferred_element_type=f32) + lax.dot_general(
        w_low, got, dims0, preferred_element_type=f32
    )
    fin_send[...] = combined.astype(bf)
    last = remote(fin_send, fin_recv, pair_sem.at[6], pair_sem.at[7], sibling)
    last.start()
    mix_ref[:, mine] = combined.astype(bf)
    last.wait()
    mix_ref[:, theirs] = fin_recv[...]

    share_sent(toks, tok_out, tok_in)
    share_sent(made, made_out, made_in)
    remote(wall.at[pl.ds(0, 7)], wall.at[pl.ds(0, 7)], qa_out.at[0], qb_in.at[0], across).wait_send()
    remote(wall.at[pl.ds(0, 24)], wall.at[pl.ds(0, 24)], qb_out.at[0], qb_in.at[0], across).wait_send()

    @pl.when(gives)
    def _():
        remote(wout.at[pl.ds(0, 7)], wout.at[pl.ds(0, 7)], oa_out.at[0], ob_in.at[0], across).wait_send()

    remote(wout.at[pl.ds(0, 12)], wout.at[pl.ds(0, 12)], ob_out.at[0], ob_in.at[0], across).wait_send()


def local(tokens, w_query, w_key, w_value, w_out, cache_keys, cache_values, parents, lengths, accepted_leaf, routes,
          route_weight, w_gateup, w_down):
    f32, bf = jnp.float32, jnp.bfloat16
    vmem = pltpu.VMEM
    keep = pl.BlockSpec(memory_space=pltpu.VMEM)
    dma = pltpu.SemaphoreType.DMA
    attended, expert_mix, new_keys, new_values = pl.pallas_call(
        layer_kernel,
        out_shape=(
            jax.ShapeDtypeStruct(tokens.shape, bf),
            jax.ShapeDtypeStruct(tokens.shape, bf),
            jax.ShapeDtypeStruct(cache_keys.shape, bf),
            jax.ShapeDtypeStruct(cache_values.shape, bf),
        ),
        in_specs=[pl.BlockSpec(memory_space=pl.ANY)] * 14,
        out_specs=(keep,) * 4,
        scratch_shapes=[
            pltpu.SMEM((2,), jnp.int32), pltpu.SMEM((2,), jnp.int32),
            vmem((2, 8, D_MODEL), bf), vmem((48, HALF), bf), vmem((48, 256), bf), vmem((48, 256), bf),
            vmem((2, 128, 256), bf), vmem((2, 128, 256), bf), vmem((2, TREE), jnp.int32), vmem((8, 16), jnp.int32),
            vmem((8, 16), f32), vmem((2, D_MODEL, 256), bf), vmem((256, D_MODEL), bf),
            vmem((8, 2, 8, D_MODEL), bf), vmem((8, PACKED, 128), bf), vmem((32, PACKED, 128), bf), vmem((32, 48, HALF), bf),
            vmem((ROWS, D_MODEL), bf), vmem((8, CARRIED, 128), bf),
            vmem((2, 4, 2, 8, HALF), bf), vmem((2, 4, 2, 8, HALF), bf), vmem((2, 4, 2, 8, 128), f32),
            vmem((2, 4, 2, 8, 128), f32), vmem((16, HALF), bf), vmem((16, HALF), bf), vmem((16, 128), f32),
            vmem((16, 128), f32), vmem((16, D_MODEL), bf), vmem((16, D_MODEL), bf),
            vmem((SLOTS, SLAB, HALF), bf), vmem((2, SLOTS, SLAB, HALF), bf), vmem((SLOTS * SLAB, HALF), bf),
            vmem((SLOTS * SLAB, HALF), bf), vmem((SLOTS, SLAB, HALF), bf), vmem((SLOTS, SLAB, HALF), bf),
            vmem((16, HALF), bf), vmem((16, HALF), bf),
            dma((14,)), dma((7,)), dma((7,)), dma((7,)), dma((7,)),
            dma((1,)), dma((8,)), dma((1,)), dma((1,)),
            dma((1,)), dma((8,)), dma((1,)), dma((4,)), dma((1,)), dma((1,)),
            dma((12,)), dma((8,)), dma((2,)), dma((2,)),
        ],
        compiler_params=pltpu.CompilerParams(
            collective_id=1, has_side_effects=True, vmem_limit_bytes=50 * 1024 * 1024
        ),
    )(
        lengths, accepted_leaf, tokens.reshape(2, 8, D_MODEL), w_query, w_key, w_value, cache_keys, cache_values, parents,
        w_out.T, routes.T, route_weight.T, w_gateup[0].transpose(1, 0, 2), w_down[0],
    )
    return (attended, expert_mix, new_keys, new_values)


def solution(mesh):
    in_specs = (
        P(("blk", "expert"), None),
        P("expert", "tp"),
        P("expert", "tp"),
        P("expert", "tp"),
        P("tp", "expert"),
        P("expert", "blk", "tp"),
        P("expert", "blk", "tp"),
        P("expert", None),
        P("expert"),
        P("expert"),
        P(("blk", "expert"), None),
        P(("blk", "expert"), None),
        P("expert", None, None, "tp"),
        P("expert", "tp", None),
    )
    out_specs = (
        P(("blk", "expert"), None),
        P(("blk", "expert"), None),
        P("expert", "blk", "tp"),
        P("expert", "blk", "tp"),
    )
    return jax.shard_map(local, mesh=mesh, in_specs=in_specs, out_specs=out_specs, check_vma=False)
```

```python
import jax
import jax.numpy as jnp
from jax import lax
from jax.experimental import pallas as pl
from jax.experimental.pallas import tpu as pltpu
from jax.sharding import PartitionSpec as P

score_scale = 0.015625
residual_scale = 0.22
masked_score = -1e30
D_MODEL = 1536
HALF = 768
SLOTS = 32
OWN_SLOT = 12
SLAB = 8
TREE = 64
ROWS = 128
CARRIED = 160
PACKED = 64
MESH = pl.DeviceIdType.MESH


def layer_kernel(len_hbm, leaf_hbm, tok_hbm, wq_hbm, wk_hbm, wv_hbm, ck_hbm, cv_hbm, par_hbm, wo_hbm, routes_hbm, weight_hbm,
                 wgu_hbm, wdn_hbm, att_ref, mix_ref, nk_ref, nv_ref, len_ref, leaf_ref, tok_ref, wq_ref, wk_ref, wv_ref,
                 ck_ref, cv_ref, par_ref, routes_ref, weight_ref, wgu, wdn, toks, slices, wall, wout, normed_ref, made,
                 part_send, near_recv, stat_send, near_stat, far_send, far_recv, far_stat_send, far_stat, pair_send,
                 pair_recv, send, recv, half_send, half_recv, back_send, back_recv, fin_send, fin_recv, load_sem, tok_out,
                 tok_in, made_out, made_in, qa_out, qa_in, qb_out, qb_in, oa_out, oa_in, ob_out, ob_in, oy_out, oy_in, part_sem,
                 pair_sem, ship_out, ship_in):
    f32, bf = jnp.float32, jnp.bfloat16
    blk = lax.axis_index("blk")
    exp = lax.axis_index("expert")
    tp = lax.axis_index("tp")
    hi = lax.div(blk, 4)
    y = lax.rem(blk, 4)
    z_lo = lax.div(exp, 4)
    z = hi * 8 + z_lo
    x = lax.rem(exp, 4)
    partner = (1 - hi) * 4 + y
    z_blk, z_exp = {}, {}
    for dz in range(-4, 5):
        zz = lax.rem(z + (dz + 16), 16)
        z_blk[dz] = lax.div(zz, 8) * 4 + y
        z_exp[dz] = lax.rem(zz, 8) * 4
    x_at = {dx: lax.rem(x + dx, 4) for dx in range(4)}
    y_at = {dy: lax.rem(y + dy, 4) for dy in range(4)}

    def plane(dz, dx):
        return (z_blk[dz], z_exp[dz] + x_at[dx], tp)

    def along_z(dz):
        return plane(dz, 0)

    def along_x(dx):
        return plane(0, dx)

    def along_y(dy):
        return (hi * 4 + y_at[dy], exp, tp)

    across = (partner, exp, tp)
    sibling = (blk, exp, 1 - tp)

    def source_row(slot):
        return lax.rem(z_lo + (11 - slot), 8) * 4 + x

    def remote(src, dst, ssem, rsem, device):
        return pltpu.make_async_remote_copy(
            src_ref=src, dst_ref=dst, send_sem=ssem, recv_sem=rsem, device_id=device, device_id_type=MESH
        )

    pairs = (
        (wq_hbm, wq_ref), (wk_hbm, wk_ref), (wv_hbm, wv_ref), (tok_hbm, tok_ref), (len_hbm, len_ref),
        (leaf_hbm, leaf_ref), (par_hbm, par_ref), (routes_hbm, routes_ref), (weight_hbm, weight_ref), (ck_hbm, ck_ref),
        (cv_hbm, cv_ref), (wo_hbm, wout.at[exp]), (wgu_hbm, wgu), (wdn_hbm, wdn),
    )
    loads = [pltpu.make_async_copy(src, dst, load_sem.at[n]) for n, (src, dst) in enumerate(pairs)]
    parity = lax.rem(y, 2)
    gives = lax.rem(z_lo + y, 2) == 0
    for n, load in enumerate(loads):
        if n == 11:
            pl.when(gives)(load.start)
        elif n < 9:
            load.start()

    barrier = pltpu.get_barrier_semaphore()

    def greet(device):
        pl.semaphore_signal(barrier, inc=1, device_id=device, device_id_type=MESH)

    for d in range(1, 8):
        greet((lax.rem(blk + d, 8), exp, tp))
    for dz in (-4, 4, -3, 3, -2, 2, -1, 1, 0):
        for dx in range(4):
            if dz or dx:
                greet(plane(dz, dx))
    greet(sibling)

    for n in range(4):
        loads[n].wait()
    group16 = lax.broadcasted_iota(jnp.int32, (16, 128), 1) // 32
    for b in range(8):
        if b < 6:
            slices[b, 0:48, :] = wq_ref[:, b * 128 : (b + 1) * 128]
        else:
            slices[b, 0:48, :] = wk_ref[:, (b - 6) * 128 : (b - 5) * 128]
        fold = jnp.zeros((16, 128), f32)
        for g in range(3):
            piece = wv_ref[16 * g : 16 * g + 16, (b // 4) * 128 : (b // 4 + 1) * 128].astype(f32)
            turn = (32 * (g - b % 4)) % 128
            piece = pltpu.roll(piece, turn, 1) if turn else piece
            fold = jnp.where(group16 == g, piece, fold)
        slices[b, 48:PACKED, :] = fold.astype(bf)
    wall[exp] = slices[blk]
    toks[blk] = tok_ref[...]
    pl.semaphore_wait(barrier, 43)

    def share_start(buf, ssem, rsem):
        remote(buf.at[blk], buf.at[blk], ssem.at[3], rsem.at[3], across).start()
        for d in range(1, 4):
            remote(buf.at[blk], buf.at[blk], ssem.at[d - 1], rsem.at[d - 1], along_y(d)).start()

    def share_forward(buf, ssem, rsem):
        remote(buf.at[partner], buf.at[partner], ssem.at[3], rsem.at[3], across).wait_recv()
        for d in range(1, 4):
            remote(buf.at[partner], buf.at[partner], ssem.at[3 + d], rsem.at[3 + d], along_y(d)).start()

    def share_finish(buf, ssem, rsem):
        for d in range(1, 4):
            for half in range(2):
                remote(
                    buf.at[blk], buf.at[(hi if half == 0 else 1 - hi) * 4 + y_at[4 - d]], ssem.at[d - 1 + 4 * half],
                    rsem.at[d - 1 + 4 * half], across,
                ).wait_recv()

    def share_sent(buf, ssem, rsem):
        for s in range(7):
            remote(buf.at[blk], buf.at[blk], ssem.at[s], rsem.at[s], across).wait_send()

    for dz in (4, -3, 3, -2, 2, -1, 1):
        remote(slices.at[z_blk[dz]], wall.at[exp], qa_out.at[0], qa_in.at[dz + 3], along_z(dz)).start()

    def pass_on(slot, buf, ssem, rsem):
        row = source_row(slot)
        for d in range(1, 4):
            remote(buf.at[row], buf.at[row], ssem.at[0], rsem.at[0], along_x(d)).start()

    share_start(toks, tok_out, tok_in)
    pass_on(3, wall, qb_out, qb_in)
    for n in (9, 10, 12, 13):
        loads[n].start()

    @pl.when(gives)
    def _():
        loads[11].wait()
        for dz in (4, -3, 3, -2, 2, -1, 1):
            remote(wout.at[exp], wout.at[exp], oa_out.at[0], oa_in.at[dz + 3], along_z(dz)).start()

    for dz in (1, -1, 2, -2, 3, -3, 4):
        row = source_row(dz + 3)
        remote(wall.at[row], wall.at[row], qa_out.at[0], qa_in.at[dz + 3], across).wait_recv()
        pass_on(dz + 3, wall, qb_out, qb_in)
    share_forward(toks, tok_out, tok_in)
    for n in range(4, 9):
        loads[n].wait()
    lane = lax.broadcasted_iota(jnp.int32, (ROWS, 128), 1)
    line = lax.broadcasted_iota(jnp.int32, (ROWS, 128), 0)
    parent = jnp.concatenate([par_ref[0:1, :], par_ref[1:2, :]], axis=1)
    parent = jnp.where(parent >= 0, parent + 64 * (lax.broadcasted_iota(jnp.int32, (1, 128), 1) // 64), -1)
    eye = jnp.where(lane == line, 1.0, 0.0)
    upward = eye + jnp.where(line == parent, 1.0, 0.0)
    for doubling in range(6):
        short = upward.astype(bf)
        upward = jnp.minimum(upward + jnp.dot(short, short, preferred_element_type=f32), 1.0)
    upward_bf = upward.astype(bf)
    dims0 = (((0,), (0,)), ((), ()))
    reach = lax.dot_general(upward_bf, eye.astype(bf), dims0, preferred_element_type=f32)
    depth = lax.dot_general(upward_bf, jnp.ones((ROWS, 128), bf), dims0, preferred_element_type=f32) - 1.0
    len0 = len_ref[0].astype(f32)
    len1 = len_ref[1].astype(f32)
    place = depth + jnp.where(line < 64, len0, len1)
    rate = jnp.exp((lane % 32).astype(f32) * (-9.210340371976184 / 32.0))
    angle = place * rate
    cos = jnp.cos(angle)
    low_half = (lane % 64) < 32
    sin = jnp.where(low_half, -1.0, 1.0) * jnp.sin(angle)
    target = jnp.sum(upward, axis=0, keepdims=True) - 1.0 + jnp.where(lane[0:1] < 64, len0, len1)
    on_path = jnp.sum(
        jnp.where((line == leaf_ref[0]) | (line == leaf_ref[1] + 64), reach, 0.0), axis=0, keepdims=True
    )

    rows = 16
    mine = pl.ds(pl.multiple_of(tp * HALF, HALF), HALF)
    theirs = pl.ds(pl.multiple_of((1 - tp) * HALF, HALF), HALF)
    slot = lax.broadcasted_iota(jnp.int32, (SLOTS * SLAB, rows), 0)
    kk = slot // SLAB
    cc = slot % SLAB
    expert_of = ((z_lo + kk // 4 + 5) % 8) * 4 + (x + kk % 4) % 4
    named = jnp.zeros((SLOTS * SLAB, rows), f32)
    weighed = jnp.zeros((SLOTS * SLAB, rows), f32)
    for t in range(8):
        hit = expert_of == routes_ref[t : t + 1, :]
        named = named + jnp.where(hit, 1.0, 0.0)
        weighed = weighed + jnp.where(hit, weight_ref[t : t + 1, :], 0.0)
    earlier = jnp.where(
        lax.broadcasted_iota(jnp.int32, (rows, rows), 0) < lax.broadcasted_iota(jnp.int32, (rows, rows), 1), 1.0, 0.0
    ).astype(bf)
    rank = jnp.dot(named.astype(bf), earlier, preferred_element_type=f32)
    chosen = jnp.where((named > 0.5) & (jnp.abs(rank - cc.astype(f32)) < 0.5), 1.0, 0.0)
    weighed = weighed * chosen
    chosen_bf = chosen.astype(bf)
    w_high = weighed.astype(bf)
    w_low = (weighed - w_high.astype(f32)).astype(bf)

    share_finish(toks, tok_out, tok_in)

    for r in range(2):
        rows = toks[:, r].reshape(TREE, D_MODEL).astype(f32)
        scale = lax.rsqrt(jnp.mean(rows * rows, axis=-1, keepdims=True) + 1e-06)
        normed_ref[r * TREE : (r + 1) * TREE, :] = (rows * scale).astype(bf)
    remote(wall.at[pl.ds(0, 24)], wall.at[pl.ds(0, 24)], qb_out.at[0], qb_in.at[0], across).wait_recv()
    w_first = wall[:, 0:48, :].reshape(D_MODEL, 128)
    folded = wall[:, 48:PACKED, :].astype(f32)
    group = lax.broadcasted_iota(jnp.int32, (32, 16, 128), 2) // 32
    w_second = jnp.concatenate([jnp.where(group == g, folded, 0.0) for g in range(3)], axis=1)
    w_second = w_second.astype(bf).reshape(D_MODEL, 128)
    first = jnp.dot(normed_ref[...], w_first, preferred_element_type=f32)
    turned = jnp.where(low_half, pltpu.roll(first, 96, 1), pltpu.roll(first, 32, 1))
    made[blk, 0:ROWS, :] = (first * cos + turned * sin).astype(bf)
    second = jnp.dot(normed_ref[...], w_second, preferred_element_type=f32)
    second = second + pltpu.roll(second, 96, 1) + pltpu.roll(second, 64, 1)
    line_group = lane[0:32] // 32
    carried = jnp.zeros((32, 128), f32)
    for q in range(4):
        piece = second[32 * q : 32 * q + 32]
        piece = pltpu.roll(piece, 32 * q, 1) if q else piece
        carried = jnp.where(line_group == q, piece, carried)
    made[blk, ROWS:CARRIED, :] = carried.astype(bf)

    share_start(made, made_out, made_in)

    for dz in (0, 1, -1, 2, -2, 3, -3, 4):
        row = source_row(dz + 3)
        source_z = lax.rem(z_lo + (8 - dz), 8)

        @pl.when(lax.rem(source_z + parity, 2) == 0)
        def _(dz=dz, row=row, source_z=source_z):
            if dz:
                remote(wout.at[row], wout.at[row], oa_out.at[0], oa_in.at[dz + 3], across).wait_recv()
            for d in range(1, 4):
                remote(
                    wout.at[row], wout.at[row], ob_out.at[0], ob_in.at[lax.div(source_z, 2)], along_x(d)
                ).start()
            near_y = (hi * 4 + lax.rem(y + 1 + 2 * lax.div(source_z, 4), 4), exp, tp)
            remote(wout.at[row], wout.at[row], oy_out.at[0], oy_in.at[0], near_y).start()

    share_forward(made, made_out, made_in)
    share_finish(made, made_out, made_in)

    for n in (9, 10):
        loads[n].wait()
    tree_k = [made[6 + c, 0:ROWS, :] for c in range(2)]
    tree_v = []
    for c in range(2):
        quarters = []
        for q in range(4):
            whole = jnp.zeros((32, 128), f32)
            for g in range(4):
                piece = made[4 * c + g, ROWS:CARRIED, :].astype(f32)
                turn = (32 * (g - q)) % 128
                piece = pltpu.roll(piece, turn, 1) if turn else piece
                whole = jnp.where(line_group == g, piece, whole)
            quarters.append(whole)
        tree_v.append(jnp.concatenate(quarters, axis=0).astype(bf))
    nt = (((1,), (1,)), ((), ()))
    left = lane < 64
    for r in range(2):
        length = len0 if r == 0 else len1
        sees = (lane[0:1] + blk * 128).astype(f32) < length
        tree_ok = (reach[r * TREE : (r + 1) * TREE] > 0.5) & (((lane[0:TREE] % 64) // 8) == blk)
        left64 = left[0:TREE]
        lane64 = lane[0:TREE]
        stat = jnp.zeros((TREE, 128), f32)
        tops = []
        for c in range(2):
            stack = []
            for head in range(6 * c, 6 * c + 6):
                block = made[head // 2, r * TREE : (r + 1) * TREE, :].astype(f32)
                side = (head // 3) % 2
                if side != head % 2:
                    block = pltpu.roll(block, 64, 1)
                stack.append(jnp.where(left64 if side == 0 else ~left64, block, 0.0).astype(bf))
            query = jnp.concatenate(stack, axis=0)
            cols = slice(c * 128, (c + 1) * 128)
            s_cache = lax.dot_general(query, ck_ref[r, :, cols], nt, preferred_element_type=f32) * score_scale
            s_tree = lax.dot_general(query, tree_k[c], nt, preferred_element_type=f32) * score_scale
            s_cache = jnp.where(sees, s_cache, masked_score).reshape(6, TREE, 128)
            s_tree = jnp.where(tree_ok, s_tree.reshape(6, TREE, 128), masked_score)
            peak = jnp.maximum(
                jnp.max(s_cache, axis=-1, keepdims=True), jnp.max(s_tree, axis=-1, keepdims=True)
            )
            p_cache = jnp.where(sees, jnp.exp(s_cache - peak), 0.0)
            p_tree = jnp.where(tree_ok, jnp.exp(s_tree - peak), 0.0)
            mass = jnp.sum(p_cache, axis=-1, keepdims=True) + jnp.sum(p_tree, axis=-1, keepdims=True)
            total = jnp.dot(
                p_cache.reshape(6 * TREE, 128).astype(bf), cv_ref[r, :, cols], preferred_element_type=f32
            ) + jnp.dot(p_tree.reshape(6 * TREE, 128).astype(bf), tree_v[c], preferred_element_type=f32)
            total = total.reshape(6, TREE, 128) / jnp.where(mass > 0.0, mass, 1.0)
            for n in range(6):
                head = 6 * c + n
                stat = jnp.where(lane64 == head, peak[n], stat)
                stat = jnp.where(lane64 == 64 + head, mass[n], stat)
                tops.append(total[n])
        for i in range(6):
            parts = []
            for u in range(2):
                head = 2 * i + u
                value = tops[head]
                if (head // 3) % 2 != u:
                    value = pltpu.roll(value, 64, 1)
                parts.append(value)
            joined = jnp.where(left64, parts[0], parts[1])
            part_send[:, :, r, :, i * 128 : (i + 1) * 128] = joined.astype(bf).reshape(2, 4, 8, 128)
        stat_send[:, :, r, :, :] = stat.reshape(2, 4, 8, 128)

    for group, other in ((0, 1 - hi), (1, hi)):
        for d in range(1, 4):
            remote(
                part_send.at[other, y_at[d]], near_recv.at[group, y], part_sem.at[4 * group], part_sem.at[4 * group + 1],
                along_y(d),
            ).start()
            remote(
                stat_send.at[other, y_at[d]], near_stat.at[group, y], part_sem.at[4 * group + 2],
                part_sem.at[4 * group + 3], along_y(d),
            ).start()
        near_recv[group, y] = part_send[other, y]
        near_stat[group, y] = stat_send[other, y]

    spread = jnp.where(
        lax.broadcasted_iota(jnp.int32, (128, HALF), 1) // 64 == lax.broadcasted_iota(jnp.int32, (128, HALF), 0), 1.0, 0.0
    ).astype(bf)

    def combine(count, stats, values):
        masses = pltpu.roll(stats.reshape(count * 16, 128), 64, 1).reshape(count, 16, 128)
        peak = jnp.max(stats, axis=0, keepdims=True)
        share = jnp.where(lane[0:16] < 12, masses * jnp.exp(stats - peak), 0.0)
        whole = jnp.sum(share, axis=0, keepdims=True)
        share = (share / jnp.where(whole > 0.0, whole, 1.0)).reshape(count * 16, 128)
        share_high = share.astype(bf)
        share_low = (share - share_high.astype(f32)).astype(bf)
        factor = jnp.dot(share_high, spread, preferred_element_type=f32) + jnp.dot(
            share_low, spread, preferred_element_type=f32
        )
        joined = jnp.sum(factor.reshape(count, 16, HALF) * values.reshape(count, 16, HALF).astype(f32), axis=0)
        stat = jnp.where(lane[0:16] < 12, peak[0], 0.0) + pltpu.roll(whole[0], 64, 1)
        return joined, stat

    def near_wait(group):
        for n, (out, into) in enumerate(((part_send.at[0], near_recv.at[group]), (stat_send.at[0], near_stat.at[group]))):
            remote(
                out.at[pl.ds(0, 3)], into.at[pl.ds(0, 3)], part_sem.at[4 * group + 2 * n],
                part_sem.at[4 * group + 2 * n + 1], across,
            ).wait()

    for g in range(4):
        remote(wout.at[pl.ds(0, 3)], wout.at[pl.ds(0, 3)], ob_out.at[0], ob_in.at[g], across).wait_recv()
        for d in range(1, 4):
            row = (2 * g + parity) * 4 + x_at[d]
            remote(wout.at[row], wout.at[row], oy_out.at[0], oy_in.at[0], along_y(1 if g < 2 else 3)).start()
    near_wait(0)
    joined, stat = combine(4, near_stat[0].reshape(4, 16, 128), near_recv[0])
    far_send[...] = joined.astype(bf)
    far_stat_send[...] = stat
    far = (
        remote(far_send, far_recv, part_sem.at[8], part_sem.at[9], across),
        remote(far_stat_send, far_stat, part_sem.at[10], part_sem.at[11], across),
    )
    for copy in far:
        copy.start()
    near_wait(1)
    joined, stat = combine(4, near_stat[1].reshape(4, 16, 128), near_recv[1])
    for copy in far:
        copy.wait()
    first_peak = stat
    second_peak = far_stat[...]
    peak = jnp.maximum(first_peak, second_peak)
    pair_share = [
        jnp.where(lane[0:16] < 12, pltpu.roll(one, 64, 1) * jnp.exp(one - peak), 0.0) for one in (first_peak, second_peak)
    ]
    whole = pair_share[0] + pair_share[1]
    inverse = 1.0 / jnp.where(whole > 0.0, whole, 1.0)
    pair_share = jnp.concatenate([pair_share[0] * inverse, pair_share[1] * inverse], axis=0)
    share_high = pair_share.astype(bf)
    share_low = (pair_share - share_high.astype(f32)).astype(bf)
    factor = jnp.dot(share_high, spread, preferred_element_type=f32) + jnp.dot(
        share_low, spread, preferred_element_type=f32
    )
    context = (factor[0:16] * joined + factor[16:32] * far_recv[...].astype(f32)).astype(bf)
    remote(wout.at[pl.ds(0, 16)], wout.at[pl.ds(0, 16)], oy_out.at[0], oy_in.at[0], across).wait()
    terms = lax.dot_general(context, wout[...].reshape(D_MODEL, HALF), nt, preferred_element_type=f32).astype(bf)
    pair_send[...] = terms
    pair = remote(pair_send, pair_recv, pair_sem.at[0], pair_sem.at[1], sibling)
    pair.start()
    pair.wait()
    attended = (terms.astype(f32) + pair_recv[...].astype(f32)).astype(bf)
    att_ref[...] = attended
    mixed = tok_ref[...].reshape(16, D_MODEL).astype(f32) + residual_scale * attended.astype(f32)
    scale = lax.rsqrt(jnp.mean(mixed * mixed, axis=-1, keepdims=True) + 1e-06)
    hidden_in = (mixed * scale).astype(bf)
    for own in range(2):

        @pl.when(tp == own)
        def _():
            sent = jnp.dot(chosen_bf, hidden_in[:, own * HALF : (own + 1) * HALF], preferred_element_type=f32).astype(bf)
            send[...] = sent.reshape(SLOTS, SLAB, HALF)

    recv[tp, OWN_SLOT] = send[OWN_SLOT]
    order = sorted(range(-3, 5), key=lambda d: -abs(d))
    for dz in order:
        for dx in (2, 1, 3, 0):
            k = (dz + 3) * 4 + dx
            if k != OWN_SLOT:
                remote(send.at[k], recv.at[tp, k], ship_out.at[0], ship_in.at[0], plane(dz, dx)).start()
    for r in range(2):
        spot = (line + blk * 128).astype(f32)
        placing = jnp.where((spot == target) & (on_path > 0.5) & ((lane // 64) == r), 1.0, 0.0)
        written = jnp.max(placing, axis=-1, keepdims=True) > 0.5
        placing = placing.astype(bf)
        for c in range(2):
            cols = slice(c * 128, (c + 1) * 128)
            moved_k = jnp.dot(placing, tree_k[c], preferred_element_type=f32)
            nk_ref[r, :, cols] = jnp.where(written, moved_k, ck_ref[r, :, cols].astype(f32)).astype(bf)
            moved_v = jnp.dot(placing, tree_v[c], preferred_element_type=f32)
            nv_ref[r, :, cols] = jnp.where(written, moved_v, cv_ref[r, :, cols].astype(f32)).astype(bf)

    remote(
        send.at[pl.ds(0, 31)], recv.at[tp, pl.ds(0, 31)], ship_out.at[0], ship_in.at[0], sibling
    ).wait()
    swap = remote(recv.at[tp], recv.at[tp], pair_sem.at[2], pair_sem.at[3], sibling)
    swap.start()
    for n in (12, 13):
        loads[n].wait()
    swap.wait()
    low = recv[0].reshape(SLOTS * SLAB, HALF)
    high = recv[1].reshape(SLOTS * SLAB, HALF)

    def proj(g):
        return jnp.dot(low, wgu[g, :HALF, :], preferred_element_type=f32) + jnp.dot(
            high, wgu[g, HALF:, :], preferred_element_type=f32
        )

    gate = proj(0)
    up = proj(1)
    hidden = (gate / (1.0 + jnp.exp(-gate)) * up).astype(bf)
    swaps = []
    half_rows = SLOTS * SLAB // 2
    for h in (1, 0):
        span = slice(h * half_rows, (h + 1) * half_rows)
        half_send[span, :] = jnp.dot(hidden[span], wdn[:, theirs], preferred_element_type=f32).astype(bf)
        swap = remote(half_send.at[span], half_recv.at[span], pair_sem.at[4 + 4 * h], pair_sem.at[5 + 4 * h], sibling)
        swap.start()
        swaps.append(swap)
    part = jnp.dot(hidden, wdn[:, mine], preferred_element_type=f32)
    for h, swap in zip((1, 0), swaps):
        span = slice(h * half_rows, (h + 1) * half_rows)
        swap.wait()
        total = (part[span] + half_recv[span, :].astype(f32)).astype(bf)
        back_send[h * 16 : h * 16 + 16] = total.reshape(16, SLAB, HALF)
        if h == 0:
            back_recv[OWN_SLOT] = total[OWN_SLOT * SLAB : (OWN_SLOT + 1) * SLAB]
        for dz in [d for d in order if (d + 3) // 4 == h]:
            for dx in (2, 1, 3, 0):
                k = (dz + 3) * 4 + dx
                if k != OWN_SLOT:
                    remote(
                        back_send.at[k], back_recv.at[k], ship_out.at[1], ship_in.at[1], plane(-dz, (4 - dx) % 4)
                    ).start()
    remote(
        back_send.at[pl.ds(0, 31)], back_recv.at[pl.ds(0, 31)], ship_out.at[1], ship_in.at[1], sibling
    ).wait()
    got = back_recv[...].reshape(SLOTS * SLAB, HALF)
    combined = lax.dot_general(w_high, got, dims0, preferred_element_type=f32) + lax.dot_general(
        w_low, got, dims0, preferred_element_type=f32
    )
    fin_send[...] = combined.astype(bf)
    last = remote(fin_send, fin_recv, pair_sem.at[6], pair_sem.at[7], sibling)
    last.start()
    mix_ref[:, mine] = combined.astype(bf)
    last.wait()
    mix_ref[:, theirs] = fin_recv[...]

    share_sent(toks, tok_out, tok_in)
    share_sent(made, made_out, made_in)
    remote(wall.at[pl.ds(0, 7)], wall.at[pl.ds(0, 7)], qa_out.at[0], qb_in.at[0], across).wait_send()
    remote(wall.at[pl.ds(0, 24)], wall.at[pl.ds(0, 24)], qb_out.at[0], qb_in.at[0], across).wait_send()

    @pl.when(gives)
    def _():
        remote(wout.at[pl.ds(0, 7)], wout.at[pl.ds(0, 7)], oa_out.at[0], ob_in.at[0], across).wait_send()

    remote(wout.at[pl.ds(0, 12)], wout.at[pl.ds(0, 12)], ob_out.at[0], ob_in.at[0], across).wait_send()


def local(tokens, w_query, w_key, w_value, w_out, cache_keys, cache_values, parents, lengths, accepted_leaf, routes,
          route_weight, w_gateup, w_down):
    f32, bf = jnp.float32, jnp.bfloat16
    vmem = pltpu.VMEM
    keep = pl.BlockSpec(memory_space=pltpu.VMEM)
    dma = pltpu.SemaphoreType.DMA
    attended, expert_mix, new_keys, new_values = pl.pallas_call(
        layer_kernel,
        out_shape=(
            jax.ShapeDtypeStruct(tokens.shape, bf),
            jax.ShapeDtypeStruct(tokens.shape, bf),
            jax.ShapeDtypeStruct(cache_keys.shape, bf),
            jax.ShapeDtypeStruct(cache_values.shape, bf),
        ),
        in_specs=[pl.BlockSpec(memory_space=pl.ANY)] * 14,
        out_specs=(keep,) * 4,
        scratch_shapes=[
            pltpu.SMEM((2,), jnp.int32), pltpu.SMEM((2,), jnp.int32),
            vmem((2, 8, D_MODEL), bf), vmem((48, HALF), bf), vmem((48, 256), bf), vmem((48, 256), bf),
            vmem((2, 128, 256), bf), vmem((2, 128, 256), bf), vmem((2, TREE), jnp.int32), vmem((8, 16), jnp.int32),
            vmem((8, 16), f32), vmem((2, D_MODEL, 256), bf), vmem((256, D_MODEL), bf),
            vmem((8, 2, 8, D_MODEL), bf), vmem((8, PACKED, 128), bf), vmem((32, PACKED, 128), bf), vmem((32, 48, HALF), bf),
            vmem((ROWS, D_MODEL), bf), vmem((8, CARRIED, 128), bf),
            vmem((2, 4, 2, 8, HALF), bf), vmem((2, 4, 2, 8, HALF), bf), vmem((2, 4, 2, 8, 128), f32),
            vmem((2, 4, 2, 8, 128), f32), vmem((16, HALF), bf), vmem((16, HALF), bf), vmem((16, 128), f32),
            vmem((16, 128), f32), vmem((16, D_MODEL), bf), vmem((16, D_MODEL), bf),
            vmem((SLOTS, SLAB, HALF), bf), vmem((2, SLOTS, SLAB, HALF), bf), vmem((SLOTS * SLAB, HALF), bf),
            vmem((SLOTS * SLAB, HALF), bf), vmem((SLOTS, SLAB, HALF), bf), vmem((SLOTS, SLAB, HALF), bf),
            vmem((16, HALF), bf), vmem((16, HALF), bf),
            dma((14,)), dma((7,)), dma((7,)), dma((7,)), dma((7,)),
            dma((1,)), dma((8,)), dma((1,)), dma((1,)),
            dma((1,)), dma((8,)), dma((1,)), dma((4,)), dma((1,)), dma((1,)),
            dma((12,)), dma((10,)), dma((2,)), dma((2,)),
        ],
        compiler_params=pltpu.CompilerParams(
            collective_id=1, has_side_effects=True, vmem_limit_bytes=50 * 1024 * 1024
        ),
    )(
        lengths, accepted_leaf, tokens.reshape(2, 8, D_MODEL), w_query, w_key, w_value, cache_keys, cache_values, parents,
        w_out.T, routes.T, route_weight.T, w_gateup[0].transpose(1, 0, 2), w_down[0],
    )
    return (attended, expert_mix, new_keys, new_values)


def solution(mesh):
    in_specs = (
        P(("blk", "expert"), None),
        P("expert", "tp"),
        P("expert", "tp"),
        P("expert", "tp"),
        P("tp", "expert"),
        P("expert", "blk", "tp"),
        P("expert", "blk", "tp"),
        P("expert", None),
        P("expert"),
        P("expert"),
        P(("blk", "expert"), None),
        P(("blk", "expert"), None),
        P("expert", None, None, "tp"),
        P("expert", "tp", None),
    )
    out_specs = (
        P(("blk", "expert"), None),
        P(("blk", "expert"), None),
        P("expert", "blk", "tp"),
        P("expert", "blk", "tp"),
    )
    return jax.shard_map(local, mesh=mesh, in_specs=in_specs, out_specs=out_specs, check_vma=False)
```

```python
import jax
import jax.numpy as jnp
from jax import lax
from jax.experimental import pallas as pl
from jax.experimental.pallas import tpu as pltpu
from jax.sharding import PartitionSpec as P

score_scale = 0.015625
residual_scale = 0.22
masked_score = -1e30
D_MODEL = 1536
HALF = 768
SLOTS = 32
OWN_SLOT = 12
SLAB = 8
TREE = 64
ROWS = 128
CARRIED = 160
PACKED = 64
MESH = pl.DeviceIdType.MESH


def layer_kernel(len_hbm, leaf_hbm, tok_hbm, wq_hbm, wk_hbm, wv_hbm, ck_hbm, cv_hbm, par_hbm, wo_hbm, routes_hbm, weight_hbm,
                 wgu_hbm, wdn_hbm, att_ref, mix_ref, nk_ref, nv_ref, len_ref, leaf_ref, tok_ref, wq_ref, wk_ref, wv_ref,
                 ck_ref, cv_ref, par_ref, routes_ref, weight_ref, wgu, wdn, toks, slices, wall, wout, normed_ref, made,
                 part_send, near_recv, stat_send, near_stat, far_send, far_recv, far_stat_send, far_stat, pair_send,
                 pair_recv, send, recv, half_send, half_recv, back_send, back_recv, fin_send, fin_recv, load_sem, tok_out,
                 tok_in, made_out, made_in, qa_out, qa_in, qb_out, qb_in, oa_out, oa_in, ob_out, ob_in, oy_out, oy_in, part_sem,
                 pair_sem, ship_out, ship_in):
    f32, bf = jnp.float32, jnp.bfloat16
    blk = lax.axis_index("blk")
    exp = lax.axis_index("expert")
    tp = lax.axis_index("tp")
    hi = lax.div(blk, 4)
    y = lax.rem(blk, 4)
    z_lo = lax.div(exp, 4)
    z = hi * 8 + z_lo
    x = lax.rem(exp, 4)
    partner = (1 - hi) * 4 + y
    z_blk, z_exp = {}, {}
    for dz in range(-4, 5):
        zz = lax.rem(z + (dz + 16), 16)
        z_blk[dz] = lax.div(zz, 8) * 4 + y
        z_exp[dz] = lax.rem(zz, 8) * 4
    x_at = {dx: lax.rem(x + dx, 4) for dx in range(4)}
    y_at = {dy: lax.rem(y + dy, 4) for dy in range(4)}

    def plane(dz, dx):
        return (z_blk[dz], z_exp[dz] + x_at[dx], tp)

    def along_z(dz):
        return plane(dz, 0)

    def along_x(dx):
        return plane(0, dx)

    def along_y(dy):
        return (hi * 4 + y_at[dy], exp, tp)

    across = (partner, exp, tp)
    sibling = (blk, exp, 1 - tp)

    def source_row(slot):
        return lax.rem(z_lo + (11 - slot), 8) * 4 + x

    def remote(src, dst, ssem, rsem, device):
        return pltpu.make_async_remote_copy(
            src_ref=src, dst_ref=dst, send_sem=ssem, recv_sem=rsem, device_id=device, device_id_type=MESH
        )

    pairs = (
        (wq_hbm, wq_ref), (wk_hbm, wk_ref), (wv_hbm, wv_ref), (tok_hbm, tok_ref), (len_hbm, len_ref),
        (leaf_hbm, leaf_ref), (par_hbm, par_ref), (routes_hbm, routes_ref), (weight_hbm, weight_ref), (ck_hbm, ck_ref),
        (cv_hbm, cv_ref), (wo_hbm, wout.at[exp]), (wgu_hbm, wgu), (wdn_hbm, wdn),
    )
    loads = [pltpu.make_async_copy(src, dst, load_sem.at[n]) for n, (src, dst) in enumerate(pairs)]
    parity = lax.rem(y, 2)
    gives = lax.rem(z_lo + y, 2) == 0
    for n, load in enumerate(loads):
        if n == 11:
            pl.when(gives)(load.start)
        elif n < 9:
            load.start()

    barrier = pltpu.get_barrier_semaphore()

    def greet(device):
        pl.semaphore_signal(barrier, inc=1, device_id=device, device_id_type=MESH)

    for d in range(1, 8):
        greet((lax.rem(blk + d, 8), exp, tp))
    for dz in (-4, 4, -3, 3, -2, 2, -1, 1, 0):
        for dx in range(4):
            if dz or dx:
                greet(plane(dz, dx))
    greet(sibling)

    for n in range(4):
        loads[n].wait()
    group16 = lax.broadcasted_iota(jnp.int32, (16, 128), 1) // 32
    for b in range(8):
        if b < 6:
            slices[b, 0:48, :] = wq_ref[:, b * 128 : (b + 1) * 128]
        else:
            slices[b, 0:48, :] = wk_ref[:, (b - 6) * 128 : (b - 5) * 128]
        fold = jnp.zeros((16, 128), f32)
        for g in range(3):
            piece = wv_ref[16 * g : 16 * g + 16, (b // 4) * 128 : (b // 4 + 1) * 128].astype(f32)
            turn = (32 * (g - b % 4)) % 128
            piece = pltpu.roll(piece, turn, 1) if turn else piece
            fold = jnp.where(group16 == g, piece, fold)
        slices[b, 48:PACKED, :] = fold.astype(bf)
    wall[exp] = slices[blk]
    toks[blk] = tok_ref[...]
    pl.semaphore_wait(barrier, 43)

    def share_start(buf, ssem, rsem):
        remote(buf.at[blk], buf.at[blk], ssem.at[3], rsem.at[3], across).start()
        for d in range(1, 4):
            remote(buf.at[blk], buf.at[blk], ssem.at[d - 1], rsem.at[d - 1], along_y(d)).start()

    def share_forward(buf, ssem, rsem):
        remote(buf.at[partner], buf.at[partner], ssem.at[3], rsem.at[3], across).wait_recv()
        for d in range(1, 4):
            remote(buf.at[partner], buf.at[partner], ssem.at[3 + d], rsem.at[3 + d], along_y(d)).start()

    def share_finish(buf, ssem, rsem):
        for d in range(1, 4):
            for half in range(2):
                remote(
                    buf.at[blk], buf.at[(hi if half == 0 else 1 - hi) * 4 + y_at[4 - d]], ssem.at[d - 1 + 4 * half],
                    rsem.at[d - 1 + 4 * half], across,
                ).wait_recv()

    def share_sent(buf, ssem, rsem):
        for s in range(7):
            remote(buf.at[blk], buf.at[blk], ssem.at[s], rsem.at[s], across).wait_send()

    for dz in (4, -3, 3, -2, 2, -1, 1):
        remote(slices.at[z_blk[dz]], wall.at[exp], qa_out.at[0], qa_in.at[dz + 3], along_z(dz)).start()

    def pass_on(slot, buf, ssem, rsem):
        row = source_row(slot)
        for d in range(1, 4):
            remote(buf.at[row], buf.at[row], ssem.at[0], rsem.at[0], along_x(d)).start()

    share_start(toks, tok_out, tok_in)
    pass_on(3, wall, qb_out, qb_in)
    for n in (9, 10, 12, 13):
        loads[n].start()

    @pl.when(gives)
    def _():
        loads[11].wait()
        for dz in (4, -3, 3, -2, 2, -1, 1):
            remote(wout.at[exp], wout.at[exp], oa_out.at[0], oa_in.at[dz + 3], along_z(dz)).start()

    for dz in (1, -1, 2, -2, 3, -3, 4):
        row = source_row(dz + 3)
        remote(wall.at[row], wall.at[row], qa_out.at[0], qa_in.at[dz + 3], across).wait_recv()
        pass_on(dz + 3, wall, qb_out, qb_in)
    share_forward(toks, tok_out, tok_in)
    for n in range(4, 9):
        loads[n].wait()
    lane = lax.broadcasted_iota(jnp.int32, (ROWS, 128), 1)
    line = lax.broadcasted_iota(jnp.int32, (ROWS, 128), 0)
    parent = jnp.concatenate([par_ref[0:1, :], par_ref[1:2, :]], axis=1)
    parent = jnp.where(parent >= 0, parent + 64 * (lax.broadcasted_iota(jnp.int32, (1, 128), 1) // 64), -1)
    eye = jnp.where(lane == line, 1.0, 0.0)
    upward = eye + jnp.where(line == parent, 1.0, 0.0)
    for doubling in range(6):
        short = upward.astype(bf)
        upward = jnp.minimum(upward + jnp.dot(short, short, preferred_element_type=f32), 1.0)
    upward_bf = upward.astype(bf)
    dims0 = (((0,), (0,)), ((), ()))
    reach = lax.dot_general(upward_bf, eye.astype(bf), dims0, preferred_element_type=f32)
    depth = lax.dot_general(upward_bf, jnp.ones((ROWS, 128), bf), dims0, preferred_element_type=f32) - 1.0
    len0 = len_ref[0].astype(f32)
    len1 = len_ref[1].astype(f32)
    place = depth + jnp.where(line < 64, len0, len1)
    rate = jnp.exp((lane % 32).astype(f32) * (-9.210340371976184 / 32.0))
    angle = place * rate
    cos = jnp.cos(angle)
    low_half = (lane % 64) < 32
    sin = jnp.where(low_half, -1.0, 1.0) * jnp.sin(angle)
    target = jnp.sum(upward, axis=0, keepdims=True) - 1.0 + jnp.where(lane[0:1] < 64, len0, len1)
    on_path = jnp.sum(
        jnp.where((line == leaf_ref[0]) | (line == leaf_ref[1] + 64), reach, 0.0), axis=0, keepdims=True
    )

    rows = 16
    mine = pl.ds(pl.multiple_of(tp * HALF, HALF), HALF)
    theirs = pl.ds(pl.multiple_of((1 - tp) * HALF, HALF), HALF)
    slot = lax.broadcasted_iota(jnp.int32, (SLOTS * SLAB, rows), 0)
    kk = slot // SLAB
    cc = slot % SLAB
    expert_of = ((z_lo + kk // 4 + 5) % 8) * 4 + (x + kk % 4) % 4
    named = jnp.zeros((SLOTS * SLAB, rows), f32)
    weighed = jnp.zeros((SLOTS * SLAB, rows), f32)
    for t in range(8):
        hit = expert_of == routes_ref[t : t + 1, :]
        named = named + jnp.where(hit, 1.0, 0.0)
        weighed = weighed + jnp.where(hit, weight_ref[t : t + 1, :], 0.0)
    earlier = jnp.where(
        lax.broadcasted_iota(jnp.int32, (rows, rows), 0) < lax.broadcasted_iota(jnp.int32, (rows, rows), 1), 1.0, 0.0
    ).astype(bf)
    rank = jnp.dot(named.astype(bf), earlier, preferred_element_type=f32)
    chosen = jnp.where((named > 0.5) & (jnp.abs(rank - cc.astype(f32)) < 0.5), 1.0, 0.0)
    weighed = weighed * chosen
    chosen_bf = chosen.astype(bf)
    w_high = weighed.astype(bf)
    w_low = (weighed - w_high.astype(f32)).astype(bf)

    share_finish(toks, tok_out, tok_in)

    for r in range(2):
        rows = toks[:, r].reshape(TREE, D_MODEL).astype(f32)
        scale = lax.rsqrt(jnp.mean(rows * rows, axis=-1, keepdims=True) + 1e-06)
        normed_ref[r * TREE : (r + 1) * TREE, :] = (rows * scale).astype(bf)
    remote(wall.at[pl.ds(0, 24)], wall.at[pl.ds(0, 24)], qb_out.at[0], qb_in.at[0], across).wait_recv()
    w_first = wall[:, 0:48, :].reshape(D_MODEL, 128)
    folded = wall[:, 48:PACKED, :].astype(f32)
    group = lax.broadcasted_iota(jnp.int32, (32, 16, 128), 2) // 32
    w_second = jnp.concatenate([jnp.where(group == g, folded, 0.0) for g in range(3)], axis=1)
    w_second = w_second.astype(bf).reshape(D_MODEL, 128)
    first = jnp.dot(normed_ref[...], w_first, preferred_element_type=f32)
    turned = jnp.where(low_half, pltpu.roll(first, 96, 1), pltpu.roll(first, 32, 1))
    made[blk, 0:ROWS, :] = (first * cos + turned * sin).astype(bf)
    second = jnp.dot(normed_ref[...], w_second, preferred_element_type=f32)
    second = second + pltpu.roll(second, 96, 1) + pltpu.roll(second, 64, 1)
    line_group = lane[0:32] // 32
    carried = jnp.zeros((32, 128), f32)
    for q in range(4):
        piece = second[32 * q : 32 * q + 32]
        piece = pltpu.roll(piece, 32 * q, 1) if q else piece
        carried = jnp.where(line_group == q, piece, carried)
    made[blk, ROWS:CARRIED, :] = carried.astype(bf)

    share_start(made, made_out, made_in)

    for dz in (0, 1, -1, 2, -2, 3, -3, 4):
        row = source_row(dz + 3)
        source_z = lax.rem(z_lo + (8 - dz), 8)

        @pl.when(lax.rem(source_z + parity, 2) == 0)
        def _(dz=dz, row=row, source_z=source_z):
            if dz:
                remote(wout.at[row], wout.at[row], oa_out.at[0], oa_in.at[dz + 3], across).wait_recv()
            for d in range(1, 4):
                remote(
                    wout.at[row], wout.at[row], ob_out.at[0], ob_in.at[lax.div(source_z, 2)], along_x(d)
                ).start()
            near_y = (hi * 4 + lax.rem(y + 1 + 2 * lax.div(source_z, 4), 4), exp, tp)
            remote(wout.at[row], wout.at[row], oy_out.at[0], oy_in.at[0], near_y).start()

    share_forward(made, made_out, made_in)
    share_finish(made, made_out, made_in)

    for n in (9, 10):
        loads[n].wait()
    tree_k = [made[6 + c, 0:ROWS, :] for c in range(2)]
    tree_v = []
    for c in range(2):
        quarters = []
        for q in range(4):
            whole = jnp.zeros((32, 128), f32)
            for g in range(4):
                piece = made[4 * c + g, ROWS:CARRIED, :].astype(f32)
                turn = (32 * (g - q)) % 128
                piece = pltpu.roll(piece, turn, 1) if turn else piece
                whole = jnp.where(line_group == g, piece, whole)
            quarters.append(whole)
        tree_v.append(jnp.concatenate(quarters, axis=0).astype(bf))
    nt = (((1,), (1,)), ((), ()))
    left = lane < 64
    for r in range(2):
        length = len0 if r == 0 else len1
        sees = (lane[0:1] + blk * 128).astype(f32) < length
        tree_ok = (reach[r * TREE : (r + 1) * TREE] > 0.5) & (((lane[0:TREE] % 64) // 8) == blk)
        left64 = left[0:TREE]
        lane64 = lane[0:TREE]
        stat = jnp.zeros((TREE, 128), f32)
        tops = []
        for c in range(2):
            stack = []
            for head in range(6 * c, 6 * c + 6):
                block = made[head // 2, r * TREE : (r + 1) * TREE, :].astype(f32)
                side = (head // 3) % 2
                if side != head % 2:
                    block = pltpu.roll(block, 64, 1)
                stack.append(jnp.where(left64 if side == 0 else ~left64, block, 0.0).astype(bf))
            query = jnp.concatenate(stack, axis=0)
            cols = slice(c * 128, (c + 1) * 128)
            s_cache = lax.dot_general(query, ck_ref[r, :, cols], nt, preferred_element_type=f32) * score_scale
            s_tree = lax.dot_general(query, tree_k[c], nt, preferred_element_type=f32) * score_scale
            s_cache = jnp.where(sees, s_cache, masked_score).reshape(6, TREE, 128)
            s_tree = jnp.where(tree_ok, s_tree.reshape(6, TREE, 128), masked_score)
            peak = jnp.maximum(
                jnp.max(s_cache, axis=-1, keepdims=True), jnp.max(s_tree, axis=-1, keepdims=True)
            )
            p_cache = jnp.where(sees, jnp.exp(s_cache - peak), 0.0)
            p_tree = jnp.where(tree_ok, jnp.exp(s_tree - peak), 0.0)
            mass = jnp.sum(p_cache, axis=-1, keepdims=True) + jnp.sum(p_tree, axis=-1, keepdims=True)
            total = jnp.dot(
                p_cache.reshape(6 * TREE, 128).astype(bf), cv_ref[r, :, cols], preferred_element_type=f32
            ) + jnp.dot(p_tree.reshape(6 * TREE, 128).astype(bf), tree_v[c], preferred_element_type=f32)
            total = total.reshape(6, TREE, 128) / jnp.where(mass > 0.0, mass, 1.0)
            for n in range(6):
                head = 6 * c + n
                stat = jnp.where(lane64 == head, peak[n], stat)
                stat = jnp.where(lane64 == 64 + head, mass[n], stat)
                tops.append(total[n])
        for i in range(6):
            parts = []
            for u in range(2):
                head = 2 * i + u
                value = tops[head]
                if (head // 3) % 2 != u:
                    value = pltpu.roll(value, 64, 1)
                parts.append(value)
            joined = jnp.where(left64, parts[0], parts[1])
            part_send[:, :, r, :, i * 128 : (i + 1) * 128] = joined.astype(bf).reshape(2, 4, 8, 128)
        stat_send[:, :, r, :, :] = stat.reshape(2, 4, 8, 128)

    def near_start(group, other):
        for d in range(1, 4):
            remote(
                part_send.at[other, y_at[d]], near_recv.at[group, y], part_sem.at[4 * group], part_sem.at[4 * group + 1],
                along_y(d),
            ).start()
            remote(
                stat_send.at[other, y_at[d]], near_stat.at[group, y], part_sem.at[4 * group + 2],
                part_sem.at[4 * group + 3], along_y(d),
            ).start()
        near_recv[group, y] = part_send[other, y]
        near_stat[group, y] = stat_send[other, y]

    near_start(0, 1 - hi)

    spread = jnp.where(
        lax.broadcasted_iota(jnp.int32, (128, HALF), 1) // 64 == lax.broadcasted_iota(jnp.int32, (128, HALF), 0), 1.0, 0.0
    ).astype(bf)

    def combine(count, stats, values):
        masses = pltpu.roll(stats.reshape(count * 16, 128), 64, 1).reshape(count, 16, 128)
        peak = jnp.max(stats, axis=0, keepdims=True)
        share = jnp.where(lane[0:16] < 12, masses * jnp.exp(stats - peak), 0.0)
        whole = jnp.sum(share, axis=0, keepdims=True)
        share = (share / jnp.where(whole > 0.0, whole, 1.0)).reshape(count * 16, 128)
        share_high = share.astype(bf)
        share_low = (share - share_high.astype(f32)).astype(bf)
        factor = jnp.dot(share_high, spread, preferred_element_type=f32) + jnp.dot(
            share_low, spread, preferred_element_type=f32
        )
        joined = jnp.sum(factor.reshape(count, 16, HALF) * values.reshape(count, 16, HALF).astype(f32), axis=0)
        stat = jnp.where(lane[0:16] < 12, peak[0], 0.0) + pltpu.roll(whole[0], 64, 1)
        return joined, stat

    def near_wait(group):
        for n, (out, into) in enumerate(((part_send.at[0], near_recv.at[group]), (stat_send.at[0], near_stat.at[group]))):
            remote(
                out.at[pl.ds(0, 3)], into.at[pl.ds(0, 3)], part_sem.at[4 * group + 2 * n],
                part_sem.at[4 * group + 2 * n + 1], across,
            ).wait()

    for g in range(4):
        remote(wout.at[pl.ds(0, 3)], wout.at[pl.ds(0, 3)], ob_out.at[0], ob_in.at[g], across).wait_recv()
        for d in range(1, 4):
            row = (2 * g + parity) * 4 + x_at[d]
            remote(wout.at[row], wout.at[row], oy_out.at[0], oy_in.at[0], along_y(1 if g < 2 else 3)).start()
    near_wait(0)
    near_start(1, hi)
    joined, stat = combine(4, near_stat[0].reshape(4, 16, 128), near_recv[0])
    far_send[...] = joined.astype(bf)
    far_stat_send[...] = stat
    far = (
        remote(far_send, far_recv, part_sem.at[8], part_sem.at[9], across),
        remote(far_stat_send, far_stat, part_sem.at[10], part_sem.at[11], across),
    )
    for copy in far:
        copy.start()
    near_wait(1)
    joined, stat = combine(4, near_stat[1].reshape(4, 16, 128), near_recv[1])
    for copy in far:
        copy.wait()
    first_peak = stat
    second_peak = far_stat[...]
    peak = jnp.maximum(first_peak, second_peak)
    pair_share = [
        jnp.where(lane[0:16] < 12, pltpu.roll(one, 64, 1) * jnp.exp(one - peak), 0.0) for one in (first_peak, second_peak)
    ]
    whole = pair_share[0] + pair_share[1]
    inverse = 1.0 / jnp.where(whole > 0.0, whole, 1.0)
    pair_share = jnp.concatenate([pair_share[0] * inverse, pair_share[1] * inverse], axis=0)
    share_high = pair_share.astype(bf)
    share_low = (pair_share - share_high.astype(f32)).astype(bf)
    factor = jnp.dot(share_high, spread, preferred_element_type=f32) + jnp.dot(
        share_low, spread, preferred_element_type=f32
    )
    context = (factor[0:16] * joined + factor[16:32] * far_recv[...].astype(f32)).astype(bf)
    remote(wout.at[pl.ds(0, 16)], wout.at[pl.ds(0, 16)], oy_out.at[0], oy_in.at[0], across).wait()
    terms = lax.dot_general(context, wout[...].reshape(D_MODEL, HALF), nt, preferred_element_type=f32).astype(bf)
    pair_send[...] = terms
    pair = remote(pair_send, pair_recv, pair_sem.at[0], pair_sem.at[1], sibling)
    pair.start()
    pair.wait()
    attended = (terms.astype(f32) + pair_recv[...].astype(f32)).astype(bf)
    att_ref[...] = attended
    mixed = tok_ref[...].reshape(16, D_MODEL).astype(f32) + residual_scale * attended.astype(f32)
    scale = lax.rsqrt(jnp.mean(mixed * mixed, axis=-1, keepdims=True) + 1e-06)
    hidden_in = (mixed * scale).astype(bf)
    for own in range(2):

        @pl.when(tp == own)
        def _():
            sent = jnp.dot(chosen_bf, hidden_in[:, own * HALF : (own + 1) * HALF], preferred_element_type=f32).astype(bf)
            send[...] = sent.reshape(SLOTS, SLAB, HALF)

    recv[tp, OWN_SLOT] = send[OWN_SLOT]
    order = sorted(range(-3, 5), key=lambda d: -abs(d))
    for dz in order:
        for dx in (2, 1, 3, 0):
            k = (dz + 3) * 4 + dx
            if k != OWN_SLOT:
                remote(send.at[k], recv.at[tp, k], ship_out.at[0], ship_in.at[0], plane(dz, dx)).start()
    for r in range(2):
        spot = (line + blk * 128).astype(f32)
        placing = jnp.where((spot == target) & (on_path > 0.5) & ((lane // 64) == r), 1.0, 0.0)
        written = jnp.max(placing, axis=-1, keepdims=True) > 0.5
        placing = placing.astype(bf)
        for c in range(2):
            cols = slice(c * 128, (c + 1) * 128)
            moved_k = jnp.dot(placing, tree_k[c], preferred_element_type=f32)
            nk_ref[r, :, cols] = jnp.where(written, moved_k, ck_ref[r, :, cols].astype(f32)).astype(bf)
            moved_v = jnp.dot(placing, tree_v[c], preferred_element_type=f32)
            nv_ref[r, :, cols] = jnp.where(written, moved_v, cv_ref[r, :, cols].astype(f32)).astype(bf)

    remote(
        send.at[pl.ds(0, 31)], recv.at[tp, pl.ds(0, 31)], ship_out.at[0], ship_in.at[0], sibling
    ).wait()
    swap = remote(recv.at[tp], recv.at[tp], pair_sem.at[2], pair_sem.at[3], sibling)
    swap.start()
    for n in (12, 13):
        loads[n].wait()
    swap.wait()
    low = recv[0].reshape(SLOTS * SLAB, HALF)
    high = recv[1].reshape(SLOTS * SLAB, HALF)

    def proj(g):
        return jnp.dot(low, wgu[g, :HALF, :], preferred_element_type=f32) + jnp.dot(
            high, wgu[g, HALF:, :], preferred_element_type=f32
        )

    gate = proj(0)
    up = proj(1)
    hidden = (gate / (1.0 + jnp.exp(-gate)) * up).astype(bf)
    swaps = []
    half_rows = SLOTS * SLAB // 2
    for h in (1, 0):
        span = slice(h * half_rows, (h + 1) * half_rows)
        half_send[span, :] = jnp.dot(hidden[span], wdn[:, theirs], preferred_element_type=f32).astype(bf)
        swap = remote(half_send.at[span], half_recv.at[span], pair_sem.at[4 + 4 * h], pair_sem.at[5 + 4 * h], sibling)
        swap.start()
        swaps.append(swap)
    part = jnp.dot(hidden, wdn[:, mine], preferred_element_type=f32)
    for h, swap in zip((1, 0), swaps):
        span = slice(h * half_rows, (h + 1) * half_rows)
        swap.wait()
        total = (part[span] + half_recv[span, :].astype(f32)).astype(bf)
        back_send[h * 16 : h * 16 + 16] = total.reshape(16, SLAB, HALF)
        if h == 0:
            back_recv[OWN_SLOT] = total[OWN_SLOT * SLAB : (OWN_SLOT + 1) * SLAB]
        for dz in [d for d in order if (d + 3) // 4 == h]:
            for dx in (2, 1, 3, 0):
                k = (dz + 3) * 4 + dx
                if k != OWN_SLOT:
                    remote(
                        back_send.at[k], back_recv.at[k], ship_out.at[1], ship_in.at[1], plane(-dz, (4 - dx) % 4)
                    ).start()
    remote(
        back_send.at[pl.ds(0, 31)], back_recv.at[pl.ds(0, 31)], ship_out.at[1], ship_in.at[1], sibling
    ).wait()
    got = back_recv[...].reshape(SLOTS * SLAB, HALF)
    combined = lax.dot_general(w_high, got, dims0, preferred_element_type=f32) + lax.dot_general(
        w_low, got, dims0, preferred_element_type=f32
    )
    fin_send[...] = combined.astype(bf)
    last = remote(fin_send, fin_recv, pair_sem.at[6], pair_sem.at[7], sibling)
    last.start()
    mix_ref[:, mine] = combined.astype(bf)
    last.wait()
    mix_ref[:, theirs] = fin_recv[...]

    share_sent(toks, tok_out, tok_in)
    share_sent(made, made_out, made_in)
    remote(wall.at[pl.ds(0, 7)], wall.at[pl.ds(0, 7)], qa_out.at[0], qb_in.at[0], across).wait_send()
    remote(wall.at[pl.ds(0, 24)], wall.at[pl.ds(0, 24)], qb_out.at[0], qb_in.at[0], across).wait_send()

    @pl.when(gives)
    def _():
        remote(wout.at[pl.ds(0, 7)], wout.at[pl.ds(0, 7)], oa_out.at[0], ob_in.at[0], across).wait_send()

    remote(wout.at[pl.ds(0, 12)], wout.at[pl.ds(0, 12)], ob_out.at[0], ob_in.at[0], across).wait_send()


def local(tokens, w_query, w_key, w_value, w_out, cache_keys, cache_values, parents, lengths, accepted_leaf, routes,
          route_weight, w_gateup, w_down):
    f32, bf = jnp.float32, jnp.bfloat16
    vmem = pltpu.VMEM
    keep = pl.BlockSpec(memory_space=pltpu.VMEM)
    dma = pltpu.SemaphoreType.DMA
    attended, expert_mix, new_keys, new_values = pl.pallas_call(
        layer_kernel,
        out_shape=(
            jax.ShapeDtypeStruct(tokens.shape, bf),
            jax.ShapeDtypeStruct(tokens.shape, bf),
            jax.ShapeDtypeStruct(cache_keys.shape, bf),
            jax.ShapeDtypeStruct(cache_values.shape, bf),
        ),
        in_specs=[pl.BlockSpec(memory_space=pl.ANY)] * 14,
        out_specs=(keep,) * 4,
        scratch_shapes=[
            pltpu.SMEM((2,), jnp.int32), pltpu.SMEM((2,), jnp.int32),
            vmem((2, 8, D_MODEL), bf), vmem((48, HALF), bf), vmem((48, 256), bf), vmem((48, 256), bf),
            vmem((2, 128, 256), bf), vmem((2, 128, 256), bf), vmem((2, TREE), jnp.int32), vmem((8, 16), jnp.int32),
            vmem((8, 16), f32), vmem((2, D_MODEL, 256), bf), vmem((256, D_MODEL), bf),
            vmem((8, 2, 8, D_MODEL), bf), vmem((8, PACKED, 128), bf), vmem((32, PACKED, 128), bf), vmem((32, 48, HALF), bf),
            vmem((ROWS, D_MODEL), bf), vmem((8, CARRIED, 128), bf),
            vmem((2, 4, 2, 8, HALF), bf), vmem((2, 4, 2, 8, HALF), bf), vmem((2, 4, 2, 8, 128), f32),
            vmem((2, 4, 2, 8, 128), f32), vmem((16, HALF), bf), vmem((16, HALF), bf), vmem((16, 128), f32),
            vmem((16, 128), f32), vmem((16, D_MODEL), bf), vmem((16, D_MODEL), bf),
            vmem((SLOTS, SLAB, HALF), bf), vmem((2, SLOTS, SLAB, HALF), bf), vmem((SLOTS * SLAB, HALF), bf),
            vmem((SLOTS * SLAB, HALF), bf), vmem((SLOTS, SLAB, HALF), bf), vmem((SLOTS, SLAB, HALF), bf),
            vmem((16, HALF), bf), vmem((16, HALF), bf),
            dma((14,)), dma((7,)), dma((7,)), dma((7,)), dma((7,)),
            dma((1,)), dma((8,)), dma((1,)), dma((1,)),
            dma((1,)), dma((8,)), dma((1,)), dma((4,)), dma((1,)), dma((1,)),
            dma((12,)), dma((10,)), dma((2,)), dma((2,)),
        ],
        compiler_params=pltpu.CompilerParams(
            collective_id=1, has_side_effects=True, vmem_limit_bytes=50 * 1024 * 1024
        ),
    )(
        lengths, accepted_leaf, tokens.reshape(2, 8, D_MODEL), w_query, w_key, w_value, cache_keys, cache_values, parents,
        w_out.T, routes.T, route_weight.T, w_gateup[0].transpose(1, 0, 2), w_down[0],
    )
    return (attended, expert_mix, new_keys, new_values)


def solution(mesh):
    in_specs = (
        P(("blk", "expert"), None),
        P("expert", "tp"),
        P("expert", "tp"),
        P("expert", "tp"),
        P("tp", "expert"),
        P("expert", "blk", "tp"),
        P("expert", "blk", "tp"),
        P("expert", None),
        P("expert"),
        P("expert"),
        P(("blk", "expert"), None),
        P(("blk", "expert"), None),
        P("expert", None, None, "tp"),
        P("expert", "tp", None),
    )
    out_specs = (
        P(("blk", "expert"), None),
        P(("blk", "expert"), None),
        P("expert", "blk", "tp"),
        P("expert", "blk", "tp"),
    )
    return jax.shard_map(local, mesh=mesh, in_specs=in_specs, out_specs=out_specs, check_vma=False)
```
